32 devices in a mesh: dp: 8 (over z, core), ctx: 4 (over y, x).
Axes of the slice: x: 2, y: 2, z: 4, core: 2. Of those that a mesh axis runs over, the one named last changes fastest.
Arguments:
- inputs: float32 [8, 512, 1024], P('dp', 'ctx'), may hold values from -6 to 6
- segments: int32 [8, 512], P('dp'), may hold values from 0 to 7, never falling along the last dimension, each value on 1 to 256 neighbouring positions
- cotangent: float32 [8, 512, 1024], P('dp', 'ctx'), may hold values from -6 to 6
- mixer_params: float32 [8192, 1024], P(('dp', 'ctx')), may hold values from -0.1875 to 0.1875
- mixer_first: float32 [8192, 1024], P(('dp', 'ctx')), may hold values from -12 to 12
- mixer_second: float32 [8192, 1024], P(('dp', 'ctx')), may hold values from 10 to 1000
- feed_params: float32 [8448, 1024], P(('dp', 'ctx')), may hold values from -0.1875 to 0.1875
- feed_first: float32 [8448, 1024], P(('dp', 'ctx')), may hold values from -12 to 12
- feed_second: float32 [8448, 1024], P(('dp', 'ctx')), may hold values from 10 to 1000
- small_params: float32 [35088], replicated, may hold values from -8 to 1.5
- small_first: float32 [35088], replicated, may hold values from -12 to 12
- small_second: float32 [35088], replicated, may hold values from 10 to 1000
Outputs:
- output: float32 [8, 512, 1024], P('dp', 'ctx')
- input_grad: float32 [8, 512, 1024], P('dp', 'ctx')
- mixer_grad: float32 [8192, 1024], P(('dp', 'ctx'))
- feed_grad: float32 [8448, 1024], P(('dp', 'ctx'))
- small_grad: float32 [35088], replicated
- mixer_new: float32 [8192, 1024], P(('dp', 'ctx'))
- mixer_moment: float32 [8192, 1024], P(('dp', 'ctx'))
- mixer_square: float32 [8192, 1024], P(('dp', 'ctx'))
- feed_new: float32 [8448, 1024], P(('dp', 'ctx'))
- feed_moment: float32 [8448, 1024], P(('dp', 'ctx'))
- feed_square: float32 [8448, 1024], P(('dp', 'ctx'))
- small_new: float32 [35088], replicated
- small_moment: float32 [35088], replicated
- small_square: float32 [35088], replicated
The draws below stay inside these ranges and needn't reach their ends.
Inputs may be any that keep to these rules, and one draw needn't show every extreme that they name: `segments`: segment numbers never fall along a sequence; a segment holds 1 to 256 tokens and in each sequence one holds exactly 256.
All inputs are finite; a program needn't handle non-finite values.
Results may differ from the reference program's by a relative error of at most 0.022.
Values may be sent and summed in bfloat16 or wider, within the bound.
A program may use at most 256 MiB of HBM per device.

```python
import math
import jax
import jax.numpy as jnp
import numpy as np
from jax import lax

D = 1024
H = 8
DK = 128
DV = 256
FF = 2816
CONV = 4
SPAN = 64
STEP = 10
LENGTH = 512
SEQS = 8
MIXROWS = 8192
MLPROWS = 8448
NSMALL = 35088


def draw_small_params(key, part):
    channels = 2 * H * DK + H * DV
    subkeys = jax.random.split(key, 5)
    conv_part = jax.random.uniform(subkeys[0], (CONV * channels,), jnp.float32, -1.0, 1.0)
    gain_part = jnp.clip(1.0 + 0.1 * jax.random.normal(subkeys[1], (2 * D + DV,), jnp.float32), 0.6, 1.4)
    bound_gate = (3.0 / D) ** 0.5
    gate_part = jax.random.uniform(subkeys[2], (2 * H * D,), jnp.float32, -bound_gate, bound_gate)
    scale_part = jax.random.uniform(subkeys[3], (H,), jnp.float32, -4.0, 0.0)
    shift_part = jax.random.uniform(subkeys[4], (H,), jnp.float32, -8.0, -2.0)
    return jnp.concatenate([conv_part, gain_part, gate_part, scale_part, shift_part])


def level_of(rng, dims, cuts, low, largest):
    def one(axis_at, shards_of):
        draws = jax.random.uniform(jax.random.fold_in(jax.random.fold_in(rng, 6), axis_at), (shards_of,), jnp.float32, low / len(cuts), largest / len(cuts))
        return jnp.repeat(jnp.exp(draws), dims[axis_at] // shards_of).reshape((-1,) + (1,) * (len(dims) - axis_at - 1))

    level = one(*cuts[0])
    for cut in cuts[1:]:
        level = level * one(*cut)
    return level


def profile(count, total, most, lean):
    loads = [(1 << 20) // math.isqrt(rank ** lean) + 1 for rank in range(2, count + 1)]
    rest, counts = total - most - (count - 1), [1] * (count - 1)
    while rest > 0:
        free = [i for i in range(count - 1) if counts[i] < most]
        whole, left = sum([loads[i] for i in free]), rest
        for i in free:
            more = min(most - counts[i], max(1, left * loads[i] // whole), rest)
            counts[i] = counts[i] + more
            rest = rest - more
    return np.array([most] + counts)


def ragged(own_key, amount, total, limit, lean):
    if amount == 2:
        one = jax.random.randint(own_key, (), max(1, total - limit), min(limit, total - 1) + 1)
        return jnp.stack([one, total - one])
    tallies = jnp.asarray(profile(amount, total, limit, lean), jnp.int32)
    pairs = (amount - 1) // 2
    donor, taker = tallies[1:1 + 2 * pairs:2], tallies[2:2 + 2 * pairs:2]
    room = jnp.minimum(donor - 1, limit - taker)
    shifted = jax.random.randint(jax.random.fold_in(own_key, 1), (pairs,), 0, 1 << 20) % (room + 1)
    tallies = tallies.at[1:1 + 2 * pairs:2].set(donor - shifted).at[2:2 + 2 * pairs:2].set(taker + shifted)
    return tallies[jax.random.permutation(jax.random.fold_in(own_key, 2), amount)]


def normal_values(rng, shape, scale, bound, cuts=(), kind=jnp.bfloat16):
    gain = level_of(rng, shape, cuts, -0.22, 0.18) if cuts else 1.0
    values = jax.random.normal(rng, shape, jnp.float32) * scale * gain
    return jnp.minimum(jnp.maximum(values, -bound), bound).astype(kind)


def setup_inputs(seed: int = 0) -> dict:
    seeds = jax.random.split(jax.random.key(seed), 13)
    inputs = normal_values(seeds[0], (SEQS, LENGTH, D), 1.0, 6.0, ((0, 8), (1, 4)), jnp.float32)
    segments = jax.vmap(lambda own: jnp.searchsorted(jnp.cumsum(ragged(own, 8, LENGTH, LENGTH // 2, 1)), jnp.arange(LENGTH), side="right"))(jax.random.split(seeds[1], SEQS)).reshape((SEQS, LENGTH)).astype(jnp.int32)
    cotangent = normal_values(seeds[2], (SEQS, LENGTH, D), 1.0, 6.0, ((0, 8), (1, 4)), jnp.float32)
    mixer_params = normal_values(seeds[3], (MIXROWS, D), D ** -0.5, 0.1875, ((0, 32),), jnp.float32)
    mixer_first = normal_values(seeds[4], (MIXROWS, D), 2.0, 12.0, ((0, 32),), jnp.float32)
    mixer_second = jnp.clip(jnp.exp(math.log(1000.0) - 4.6051702 * jax.random.uniform(seeds[5], (MIXROWS, D), jnp.float32) ** level_of(seeds[5], (MIXROWS, D), ((0, 32),), -0.2, 0.2)), 10.0, 1000.0)
    feed_params = normal_values(seeds[6], (MLPROWS, D), D ** -0.5, 0.1875, ((0, 32),), jnp.float32)
    feed_first = normal_values(seeds[7], (MLPROWS, D), 2.0, 12.0, ((0, 32),), jnp.float32)
    feed_second = jnp.clip(jnp.exp(math.log(1000.0) - 4.6051702 * jax.random.uniform(seeds[8], (MLPROWS, D), jnp.float32) ** level_of(seeds[8], (MLPROWS, D), ((0, 32),), -0.2, 0.2)), 10.0, 1000.0)
    small_params = draw_small_params(jax.random.fold_in(seeds[12], 71), 0)
    small_first = normal_values(seeds[10], (NSMALL,), 2.0, 12.0, (), jnp.float32)
    small_second = jnp.clip(jnp.exp(jax.random.uniform(seeds[11], (NSMALL,), jnp.float32, math.log(10.0), math.log(1000.0))), 10.0, 1000.0)
    return dict(inputs=inputs, segments=segments, cotangent=cotangent, mixer_params=mixer_params, mixer_first=mixer_first, mixer_second=mixer_second, feed_params=feed_params, feed_first=feed_first, feed_second=feed_second, small_params=small_params, small_first=small_first, small_second=small_second)


PRECISE = lax.Precision.HIGHEST
EPS_NORM = 1e-06
EPS_GATE = 1e-05
EPS_KEYS = 1e-06
LEARN_RATE = 0.002
FIRST_RATE = 0.9
SECOND_RATE = 0.95
EPS_ADAM = 1e-08
WEIGHT_DECAY = 0.1

def span_step(memory, queries, key_rows, value_rows, beta_rows, log_decay, segment_ids, segment_before):
    extent = segment_ids.shape[0]
    places = jnp.arange(extent)
    lower_mask = places[:, None] >= places[None, :]
    strict_mask = places[:, None] > places[None, :]
    shared = (segment_ids[:, None] == segment_ids[None, :]) & lower_mask
    running = jnp.cumsum(log_decay, axis=1)
    spread = jnp.minimum(running[:, :, None] - running[:, None, :], 0.0)
    decays = jnp.where(shared[None], jnp.exp(spread), 0.0)
    carried = jnp.where((segment_ids == segment_before)[None, :], jnp.exp(running), 0.0)
    key_key = jnp.einsum('hti,hsi->hts', key_rows, key_rows, precision=PRECISE)
    couple = jnp.where(strict_mask[None], decays * beta_rows[:, None, :] * key_key, 0.0)
    system = couple + jnp.eye(extent, dtype=couple.dtype)
    target = value_rows - carried[:, :, None] * jnp.einsum('hti,hiw->htw', key_rows, memory, precision=PRECISE)
    deltas = lax.linalg.triangular_solve(system, target, left_side=True, lower=True, unit_diagonal=True)
    query_key = jnp.einsum('hti,hsi->hts', queries, key_rows, precision=PRECISE)
    mixing = decays * beta_rows[:, None, :] * query_key
    outputs = carried[:, :, None] * jnp.einsum('hti,hiw->htw', queries, memory, precision=PRECISE)
    outputs = outputs + jnp.einsum('hts,hsw->htw', mixing, deltas, precision=PRECISE)
    last_weight = decays[:, -1, :] * beta_rows
    updated = carried[:, -1][:, None, None] * memory
    updated = updated + jnp.einsum('hsi,hsw->hiw', key_rows * last_weight[:, :, None], deltas, precision=PRECISE)
    return (outputs, updated)

def delta_rule(memory, queries, key_rows, value_rows, beta_rows, log_decay, segment_ids, segment_before):
    head_count = queries.shape[0]
    token_count = queries.shape[1]
    block_count = token_count // SPAN

    def blocks(tensor):
        shaped = tensor.reshape((head_count, block_count, SPAN) + tensor.shape[2:])
        return jnp.moveaxis(shaped, 1, 0)
    segment_blocks = segment_ids.reshape(block_count, SPAN)
    befores = jnp.concatenate([jnp.reshape(segment_before, (1,)), segment_blocks[:-1, -1]])

    def advance(carry_state, pieces):
        outputs, carry_state = span_step(carry_state, *pieces)
        return (carry_state, outputs)
    final_state, outputs = lax.scan(advance, memory, (blocks(queries), blocks(key_rows), blocks(value_rows), blocks(beta_rows), blocks(log_decay), segment_blocks, befores))
    value_width = value_rows.shape[-1]
    return (jnp.moveaxis(outputs, 0, 1).reshape(head_count, token_count, value_width), final_state)

def mixer_inputs(extended, conv_weight, beta_logit, alpha_logit, decay_log, decay_bias, segment_wide):
    margin = CONV - 1
    token_count = extended.shape[0] - margin
    segment_ids = segment_wide[margin:]
    mixed = jnp.zeros((token_count, extended.shape[1]), extended.dtype)
    for offset in range(CONV):
        start_row = margin - offset
        window = extended[start_row:start_row + token_count]
        keep_mask = (segment_wide[start_row:start_row + token_count] == segment_ids)[:, None]
        mixed = mixed + jnp.where(keep_mask, window * conv_weight[offset], 0.0)
    active = jax.nn.silu(mixed)
    key_width = H * DK
    queries = active[:, :key_width].reshape(token_count, H, DK)
    key_rows = active[:, key_width:2 * key_width].reshape(token_count, H, DK)
    value_rows = active[:, 2 * key_width:].reshape(token_count, H, DV)
    queries = queries * lax.rsqrt(lax.optimization_barrier(jnp.sum(queries * queries, axis=-1, keepdims=True)) + EPS_KEYS) * DK ** (-0.5)
    key_rows = key_rows * lax.rsqrt(lax.optimization_barrier(jnp.sum(key_rows * key_rows, axis=-1, keepdims=True)) + EPS_KEYS)
    beta_rows = jax.nn.sigmoid(beta_logit)
    log_decay = -jnp.exp(decay_log) * jax.nn.softplus(alpha_logit + decay_bias)
    return (jnp.moveaxis(queries, 1, 0), jnp.moveaxis(key_rows, 1, 0), jnp.moveaxis(value_rows, 1, 0), beta_rows.T, log_decay.T)

def gated_norm(outputs, gate_pre, out_gain):
    token_count = outputs.shape[1]
    rows_major = jnp.moveaxis(outputs, 0, 1)
    scaled = rows_major * lax.rsqrt(lax.optimization_barrier(jnp.mean(rows_major * rows_major, axis=-1, keepdims=True)) + EPS_GATE) * out_gain
    gating = jax.nn.silu(gate_pre).reshape(token_count, H, DV)
    return (scaled * gating).reshape(token_count, H * DV)

def norm_back(values, inverse, gain_row, upstream):
    weighted = gain_row * upstream
    return inverse * weighted - values * inverse ** 3 * lax.optimization_barrier(jnp.mean(weighted * values, axis=-1, keepdims=True))

def unpack_small(packed):
    channels = 2 * H * DK + H * DV
    bounds = [CONV * channels, D, D, DV, 2 * H * D, H, H]
    pieces = []
    cursor = 0
    for extent in bounds:
        pieces.append(packed[cursor:cursor + extent])
        cursor = cursor + extent
    return (pieces[0].reshape(CONV, channels), pieces[1], pieces[2], pieces[3], pieces[4].reshape(2 * H, D), pieces[5], pieces[6])

def adamw(current, gradient, moment, square):
    moment = FIRST_RATE * moment + (1.0 - FIRST_RATE) * gradient
    square = SECOND_RATE * square + (1.0 - SECOND_RATE) * gradient * gradient
    update = moment / (1.0 - FIRST_RATE ** STEP) / (jnp.sqrt(square / (1.0 - SECOND_RATE ** STEP)) + EPS_ADAM)
    return (current - LEARN_RATE * (update + WEIGHT_DECAY * current), moment, square)

def sequence_pass(row_inputs, segment_row, row_cotangent, mixer_weights, feed_weights, smalls):
    conv_weight, gain_first, gain_second, out_gain, gate_rows, decay_log, decay_bias = smalls
    channels = 2 * H * DK + H * DV
    input_rows = channels + H * DV
    margin = CONV - 1
    in_weight = mixer_weights[:input_rows]
    out_weight = mixer_weights[input_rows:]
    up_weight = feed_weights[:2 * FF]
    down_weight = feed_weights[2 * FF:]
    inverse_first = lax.rsqrt(lax.optimization_barrier(jnp.mean(row_inputs * row_inputs, axis=-1, keepdims=True)) + EPS_NORM)
    normed = (row_inputs * inverse_first * gain_first).astype(jnp.bfloat16)
    projected = jnp.dot(normed.astype(jnp.float32), in_weight.T.astype(jnp.float32), preferred_element_type=jnp.float32)
    conv_input = projected[:, :channels].astype(jnp.bfloat16)
    gate_pre = projected[:, channels:]
    gate_half = gate_rows.astype(jnp.bfloat16)
    logits = jnp.dot(normed.astype(jnp.float32), gate_half.T.astype(jnp.float32), preferred_element_type=jnp.float32)

    def mixer_map(conv_float, gate_value, beta_logit, alpha_logit, conv_taps, gain_out, decay_scale, decay_shift):
        extended = jnp.concatenate([jnp.zeros((margin, channels), conv_float.dtype), conv_float])
        segment_wide = jnp.concatenate([jnp.full((margin,), -1, jnp.int32), segment_row])
        prepared = mixer_inputs(extended, conv_taps, beta_logit, alpha_logit, decay_scale, decay_shift, segment_wide)
        memory = jnp.zeros((H, DK, DV), conv_float.dtype)
        outputs, _ = delta_rule(memory, prepared[0], prepared[1], prepared[2], prepared[3], prepared[4], segment_row, jnp.full((), -1, jnp.int32))
        return gated_norm(outputs, gate_value, gain_out)
    normed_mix, mixer_back = jax.vjp(mixer_map, conv_input.astype(jnp.float32), gate_pre, logits[:, :H], logits[:, H:], conv_weight, out_gain, decay_log, decay_bias)
    mix_half = normed_mix.astype(jnp.bfloat16)
    hidden = row_inputs + jnp.dot(mix_half.astype(jnp.float32), out_weight.astype(jnp.float32), preferred_element_type=jnp.float32)
    inverse_second = lax.rsqrt(lax.optimization_barrier(jnp.mean(hidden * hidden, axis=-1, keepdims=True)) + EPS_NORM)
    hidden_normed = (hidden * inverse_second * gain_second).astype(jnp.bfloat16)
    gate_up = jnp.dot(hidden_normed.astype(jnp.float32), up_weight.T.astype(jnp.float32), preferred_element_type=jnp.float32)
    gate_part = gate_up[:, :FF]
    up_part = gate_up[:, FF:]
    middle = (jax.nn.silu(gate_part) * up_part).astype(jnp.bfloat16)
    result = hidden + jnp.dot(middle.astype(jnp.float32), down_weight.astype(jnp.float32), preferred_element_type=jnp.float32)
    cotangent_half = row_cotangent.astype(jnp.bfloat16)
    grad_middle = jnp.dot(cotangent_half.astype(jnp.float32), down_weight.T.astype(jnp.float32), preferred_element_type=jnp.float32)
    sigmoid_gate = jax.nn.sigmoid(gate_part)
    grad_gate = grad_middle * up_part * (sigmoid_gate + gate_part * sigmoid_gate * (1.0 - sigmoid_gate))
    grad_up = grad_middle * gate_part * sigmoid_gate
    grad_gate_up = jnp.concatenate([grad_gate, grad_up], axis=1).astype(jnp.bfloat16)
    grad_hidden_normed = jnp.dot(grad_gate_up.astype(jnp.float32), up_weight.astype(jnp.float32), preferred_element_type=jnp.float32)
    grad_hidden = row_cotangent + norm_back(hidden, inverse_second, gain_second, grad_hidden_normed)
    grad_gain_second = lax.optimization_barrier(jnp.sum(grad_hidden_normed * hidden * inverse_second, axis=0))
    grad_hidden_half = grad_hidden.astype(jnp.bfloat16)
    grad_mix = jnp.dot(grad_hidden_half.astype(jnp.float32), out_weight.T.astype(jnp.float32), preferred_element_type=jnp.float32)
    back = mixer_back(grad_mix)
    grad_projected = jnp.concatenate([back[0], back[1]], axis=1).astype(jnp.bfloat16)
    grad_logits = jnp.concatenate([back[2], back[3]], axis=1).astype(jnp.bfloat16)
    grad_normed = jnp.dot(grad_projected.astype(jnp.float32), in_weight.astype(jnp.float32), preferred_element_type=jnp.float32)
    grad_normed = grad_normed + jnp.dot(grad_logits.astype(jnp.float32), gate_half.astype(jnp.float32), preferred_element_type=jnp.float32)
    grad_inputs = grad_hidden + norm_back(row_inputs, inverse_first, gain_first, grad_normed)
    grad_gain_first = lax.optimization_barrier(jnp.sum(grad_normed * row_inputs * inverse_first, axis=0))
    mixer_grad = jnp.concatenate([jnp.dot(grad_projected.T.astype(jnp.float32), normed.astype(jnp.float32), preferred_element_type=jnp.float32), jnp.dot(mix_half.T.astype(jnp.float32), grad_hidden_half.astype(jnp.float32), preferred_element_type=jnp.float32)])
    feed_grad = jnp.concatenate([jnp.dot(grad_gate_up.T.astype(jnp.float32), hidden_normed.astype(jnp.float32), preferred_element_type=jnp.float32), jnp.dot(middle.T.astype(jnp.float32), cotangent_half.astype(jnp.float32), preferred_element_type=jnp.float32)])
    gate_grad = jnp.dot(grad_logits.T.astype(jnp.float32), normed.astype(jnp.float32), preferred_element_type=jnp.float32)
    small_grad = jnp.concatenate([back[4].reshape(-1), grad_gain_first, grad_gain_second, back[5], gate_grad.reshape(-1), back[6], back[7]])
    return (result, grad_inputs, mixer_grad, feed_grad, small_grad)

def reference(inputs, segments, cotangent, mixer_params, mixer_first, mixer_second, feed_params, feed_first, feed_second, small_params, small_first, small_second):
    mixer_weights = mixer_params.astype(jnp.bfloat16)
    feed_weights = feed_params.astype(jnp.bfloat16)
    smalls = unpack_small(small_params)

    def visit_row(totals, pieces):
        result, grad_inputs, mixer_part, feed_part, small_part = sequence_pass(pieces[0], pieces[1], pieces[2], mixer_weights, feed_weights, smalls)
        totals = (totals[0] + mixer_part, totals[1] + feed_part, totals[2] + small_part)
        return (totals, (result, grad_inputs))
    start_totals = (jnp.zeros(mixer_params.shape, jnp.float32), jnp.zeros(feed_params.shape, jnp.float32), jnp.zeros(small_params.shape, jnp.float32))
    totals, rows_out = lax.scan(visit_row, start_totals, (inputs, segments, cotangent))
    mixer_grad, feed_grad, small_grad = totals
    mixer_new, mixer_moment, mixer_square = adamw(mixer_params, mixer_grad, mixer_first, mixer_second)
    feed_new, feed_moment, feed_square = adamw(feed_params, feed_grad, feed_first, feed_second)
    small_new, small_moment, small_square = adamw(small_params, small_grad, small_first, small_second)
    return (rows_out[0], rows_out[1], mixer_grad, feed_grad, small_grad, mixer_new, mixer_moment, mixer_square, feed_new, feed_moment, feed_square, small_new, small_moment, small_square)
```

```python
import functools
import heapq

import jax
import jax.numpy as jnp
from jax import lax
from jax.experimental import pallas as pl
from jax.experimental.pallas import tpu as pltpu
from jax.sharding import PartitionSpec as P

D = 1024
H = 8
DK = 128
DV = 256
FF = 2816
CONV = 4
SPAN = 128
GROUP = 4
STEP = 10


PRECISE = lax.Precision.HIGHEST
CORE = lax.Precision.DEFAULT
EPS_NORM = 1e-06
EPS_GATE = 1e-05
EPS_KEYS = 1e-06
LEARN_RATE = 0.002
FIRST_RATE = 0.9
SECOND_RATE = 0.95
EPS_ADAM = 1e-08
WEIGHT_DECAY = 0.1


def passed_along(shard, axis, by):
    count = lax.axis_size(axis)
    pairs = [(i, i + by) for i in range(count) if 0 <= i + by < count]
    return lax.ppermute(shard, axis, pairs)


def dot(left, right, contract=((1,), (0,)), precision=None):
    return lax.dot_general(
        left, right, (contract, ((), ())), precision=precision, preferred_element_type=jnp.float32
    )


def unit_rows(raw, scale):
    inverse = lax.rsqrt(jnp.sum(raw * raw, axis=-1, keepdims=True) + EPS_KEYS)
    return (raw * (inverse * scale), inverse)


def unit_back(raw, inverse, scale, upstream):
    upstream = upstream * scale
    shared = jnp.sum(raw * upstream, axis=-1, keepdims=True)
    return inverse * upstream - raw * (inverse * inverse * inverse * shared)


def block_decays(rows, columns, extent):
    places = lax.broadcasted_iota(jnp.int32, (extent, extent), 0)
    others = lax.broadcasted_iota(jnp.int32, (extent, extent), 1)
    keep = (columns[:, 2:3] == rows[2:3, :]) & (places >= others)
    spread = jnp.minimum(columns[:, 1:2] - rows[1:2, :], 0.0)
    return (jnp.where(keep, jnp.exp(spread), 0.0), places, others)


def block_kernel(
    q_ref, k_ref, v_ref, row_ref, column_ref,
    inverse_ref, w_ref, u_ref, r_ref, o_ref, transfer_ref, offset_ref,
):
    group = row_ref.shape[0]
    extent = q_ref.shape[0]
    systems, solved, pieces = ([], [], [])
    for h in range(group):
        rows, columns = (row_ref[h, 0], column_ref[h, 0])
        keys = slice(h * DK, (h + 1) * DK)
        queries, _ = unit_rows(q_ref[:, keys], DK ** (-0.5))
        key_rows, _ = unit_rows(k_ref[:, keys], 1.0)
        decays, places, others = block_decays(rows, columns, extent)
        weighted = decays * rows[0:1, :]
        key_key = dot(key_rows, key_rows, ((1,), (1,)), CORE)
        system = jnp.where(places > others, weighted * key_key, 0.0)
        apart = places ^ others
        systems.append(system)
        solved.append(
            jnp.where(places == others, 1.0, 0.0) - jnp.where(apart < 2, system, 0.0)
        )
        mixing = weighted * dot(queries, key_rows, ((1,), (1,)), CORE)
        pieces.append((queries, key_rows, mixing, columns))
    size = 2
    while size < extent:
        level = (apart >= size) & (apart < 2 * size)
        halves = [
            dot(solved[h], jnp.where(level, systems[h], 0.0), precision=PRECISE)
            for h in range(group)
        ]
        solved = [
            solved[h] - dot(halves[h], solved[h], precision=PRECISE) for h in range(group)
        ]
        size = 2 * size
    for h in range(group):
        queries, key_rows, mixing, columns = pieces[h]
        keys = slice(h * DK, (h + 1) * DK)
        values = slice(h * DV, (h + 1) * DV)
        carried = columns[:, 3:4]
        inverse_ref[0, h] = solved[h]
        w_part = dot(solved[h], carried * key_rows, precision=CORE)
        u_part = dot(solved[h], v_ref[:, values], precision=CORE)
        w_ref[:, keys] = w_part
        u_ref[:, values] = u_part
        r_ref[:, keys] = carried * queries - dot(mixing, w_part, precision=CORE)
        o_ref[:, values] = dot(mixing, u_part, precision=CORE)
        last_keys = key_rows * columns[:, 4:5]
        rank = lax.broadcasted_iota(jnp.int32, (DK, DK), 0)
        file = lax.broadcasted_iota(jnp.int32, (DK, DK), 1)
        transfer_ref[0, h] = jnp.where(
            rank == file, carried[extent - 1 : extent, :], 0.0
        ) - dot(last_keys, w_part, ((0,), (0,)), CORE)
        offset_ref[0, h] = dot(last_keys, u_part, ((0,), (0,)), CORE)


def output_kernel(r_ref, o_ref, state_ref, gate_ref, gain_ref, recurrent_ref, mix_ref):
    for h in range(state_ref.shape[1]):
        keys = slice(h * DK, (h + 1) * DK)
        values = slice(h * DV, (h + 1) * DV)
        recurrent = o_ref[:, values] + dot(r_ref[:, keys], state_ref[0, h], precision=CORE)
        recurrent_ref[:, values] = recurrent
        inverse = lax.rsqrt(jnp.mean(recurrent * recurrent, axis=-1, keepdims=True) + EPS_GATE)
        mix_ref[:, values] = (
            recurrent * inverse * gain_ref[...] * jax.nn.silu(gate_ref[:, values])
        ).astype(jnp.bfloat16)


def gate_back_kernel(
    mix_ref, recurrent_ref, gate_ref, gain_ref, r_ref,
    grad_ref, grad_gate_ref, grad_gain_ref, local_ref,
):
    total = jnp.zeros((1, DV), jnp.float32)
    for h in range(local_ref.shape[1]):
        keys = slice(h * DK, (h + 1) * DK)
        values = slice(h * DV, (h + 1) * DV)
        upstream, recurrent, gate = (mix_ref[:, values], recurrent_ref[:, values], gate_ref[:, values])
        inverse = lax.rsqrt(jnp.mean(recurrent * recurrent, axis=-1, keepdims=True) + EPS_GATE)
        normal = recurrent * inverse
        sig = jax.nn.sigmoid(gate)
        gain = gain_ref[...]
        grad_gate_ref[:, values] = upstream * normal * gain * (sig + gate * sig * (1.0 - sig))
        scaled = upstream * (gate * sig)
        total = total + jnp.sum(scaled * normal, axis=0, keepdims=True)
        scaled = scaled * gain
        grad = inverse * (scaled - normal * jnp.mean(scaled * normal, axis=-1, keepdims=True))
        grad_ref[:, values] = grad
        local_ref[0, h] = dot(r_ref[:, keys], grad, ((0,), (0,)), CORE)
    grad_gain_ref[0] = total


def block_back_kernel(
    q_ref, k_ref, v_ref, row_ref, column_ref, inverse_ref, w_ref, u_ref, state_ref, grad_ref, next_ref,
    grad_q_ref, grad_k_ref, grad_v_ref, grad_row_ref, grad_column_ref,
):
    group = row_ref.shape[0]
    extent = q_ref.shape[0]
    for h in range(group):
        rows, columns = (row_ref[h, 0], column_ref[h, 0])
        keys = slice(h * DK, (h + 1) * DK)
        values = slice(h * DV, (h + 1) * DV)
        raw_q, raw_k = (q_ref[:, keys], k_ref[:, keys])
        queries, inverse_q = unit_rows(raw_q, DK ** (-0.5))
        key_rows, inverse_k = unit_rows(raw_k, 1.0)
        decays, places, others = block_decays(rows, columns, extent)
        beta = rows[0:1, :]
        carried, last = (columns[:, 3:4], columns[:, 4:5])
        weighted = decays * beta
        strict = places > others
        key_key = dot(key_rows, key_rows, ((1,), (1,)), CORE)
        query_key = dot(queries, key_rows, ((1,), (1,)), CORE)
        state, upstream, after = (state_ref[0, h], grad_ref[:, values], next_ref[0, h])
        delta = u_ref[:, values] - dot(w_ref[:, keys], state, precision=CORE)
        grad_delta = dot(weighted * query_key, upstream, ((0,), (0,)), CORE) + dot(
            key_rows * last, after, precision=CORE
        )
        grad_mixing = dot(upstream, delta, ((1,), (1,)), CORE)
        grad_target = dot(inverse_ref[0, h], grad_delta, ((0,), (0,)), CORE)
        grad_system = jnp.where(strict, -dot(grad_target, delta, ((1,), (1,)), CORE), 0.0)
        up_state = dot(upstream, state, ((1,), (1,)), CORE)
        down_state = dot(grad_target, state, ((1,), (1,)), CORE)
        grad_last = dot(delta, after, ((1,), (1,)), CORE)
        grad_carried = jnp.sum(up_state * queries - down_state * key_rows, axis=-1, keepdims=True)
        line = lax.broadcasted_iota(jnp.int32, (extent, 1), 0)
        grad_carried = grad_carried + jnp.where(
            line == extent - 1, jnp.sum(after * state, keepdims=True), 0.0
        )
        grad_qk = grad_mixing * weighted
        grad_kk = grad_system * weighted
        grad_queries = carried * up_state + dot(grad_qk, key_rows, precision=CORE)
        grad_keys = (
            grad_last * last
            - carried * down_state
            + dot(grad_qk, queries, ((0,), (0,)), CORE)
            + dot(grad_kk, key_rows, precision=CORE)
            + dot(grad_kk, key_rows, ((0,), (0,)), CORE)
        )
        grad_q_ref[:, keys] = unit_back(raw_q, inverse_q, DK ** (-0.5), grad_queries)
        grad_k_ref[:, keys] = unit_back(raw_k, inverse_k, 1.0, grad_keys)
        grad_v_ref[:, values] = grad_target
        spread = (grad_system * key_key + grad_mixing * query_key) * decays
        grad_row_ref[h, 0] = jnp.zeros_like(rows)
        grad_row_ref[h, 0, 0:1, :] = jnp.sum(spread, axis=0, keepdims=True)
        grad_row_ref[h, 0, 1:2, :] = -jnp.sum(spread * beta, axis=0, keepdims=True)
        place = lax.broadcasted_iota(jnp.int32, (extent, 8), 1)
        grad_column_ref[h, 0] = jnp.where(
            place == 1,
            jnp.sum(spread * beta, axis=-1, keepdims=True),
            jnp.where(
                place == 3,
                grad_carried,
                jnp.where(
                    place == 4, jnp.sum(grad_last * key_rows, axis=-1, keepdims=True), 0.0
                ),
            ),
        )


def block_scalars(beta_logit, alpha_logit, decay_log, decay_bias, segment_ids, segment_before, span):
    token_count = beta_logit.shape[0]
    count = token_count // span
    beta = jax.nn.sigmoid(beta_logit)
    log_decay = -jnp.exp(decay_log) * jax.nn.softplus(alpha_logit + decay_bias)

    def blocks(tensor):
        return tensor.T.reshape(H, count, span)

    beta, log_decay = (blocks(beta), blocks(log_decay))
    segment_blocks = segment_ids.reshape(count, span)
    befores = jnp.concatenate([jnp.reshape(segment_before, (1,)), segment_blocks[:-1, -1]])
    upper = (jnp.arange(span)[:, None] <= jnp.arange(span)[None, :]).astype(jnp.float32)
    running = jnp.einsum("hcs,st->hct", log_decay, upper, precision=PRECISE)
    carried = jnp.where((segment_blocks == befores[:, None])[None], jnp.exp(running), 0.0)
    ending = (segment_blocks == segment_blocks[:, -1:])[None]
    last = jnp.where(ending, jnp.exp(jnp.minimum(running[:, :, -1:] - running, 0.0)), 0.0) * beta
    return (beta, running, carried, last)


def kernel_call(body, grid, args, in_specs, outs, out_specs):
    return pl.pallas_call(
        body,
        grid=grid,
        in_specs=in_specs,
        out_specs=out_specs,
        out_shape=[jax.ShapeDtypeStruct(shape, dtype) for shape, dtype in outs],
        compiler_params=pltpu.CompilerParams(vmem_limit_bytes=48 * 1024 * 1024),
    )(*args)


def active_rows(extended, conv_weight, segment_wide):
    margin = CONV - 1
    token_count = extended.shape[0] - margin
    segment_ids = segment_wide[margin:]
    mixed = jnp.zeros((token_count, extended.shape[1]), extended.dtype)
    for offset in range(CONV):
        start_row = margin - offset
        window = extended[start_row : start_row + token_count]
        keep_mask = (segment_wide[start_row : start_row + token_count] == segment_ids)[:, None]
        mixed = mixed + jnp.where(keep_mask, window * conv_weight[offset], 0.0)
    return jax.nn.silu(mixed)


def norm_back(values, inverse, gain_row, upstream):
    weighted = gain_row * upstream
    return inverse * weighted - values * inverse**3 * jnp.mean(
        weighted * values, axis=-1, keepdims=True
    )


def unpack_small(packed):
    channels = 2 * H * DK + H * DV
    bounds = [CONV * channels, D, D, DV, 2 * H * D, H, H]
    pieces = []
    cursor = 0
    for extent in bounds:
        pieces.append(packed[cursor : cursor + extent])
        cursor = cursor + extent
    return (
        pieces[0].reshape(CONV, channels),
        pieces[1],
        pieces[2],
        pieces[3],
        pieces[4].reshape(2 * H, D),
        pieces[5],
        pieces[6],
    )


def adamw(current, gradient, moment, square):
    moment = FIRST_RATE * moment + (1.0 - FIRST_RATE) * gradient
    square = SECOND_RATE * square + (1.0 - SECOND_RATE) * gradient * gradient
    update = (
        moment
        / (1.0 - FIRST_RATE**STEP)
        / (jnp.sqrt(square / (1.0 - SECOND_RATE**STEP)) + EPS_ADAM)
    )
    return (current - LEARN_RATE * (update + WEIGHT_DECAY * current), moment, square)


def owner_rows(first_left, first_right, second_left, second_right):
    def product(left_part, right_part):
        return jnp.einsum(
            "tr,td->rd", left_part, right_part, preferred_element_type=jnp.float32
        ).astype(jnp.bfloat16)

    return jnp.concatenate(
        [product(first_left, first_right), product(second_left, second_right)], axis=0
    )


def to_owners(rows):
    return lax.psum_scatter(rows, ("dp", "ctx"), scatter_dimension=0, tiled=True).astype(
        jnp.float32
    )


def ranks_of(extent):
    return [0] + [side * step for step in range(1, extent) for side in (1, -1)]


def route_slots(order, extents):
    found = [{}]
    for dim in order:
        values = ranks_of(extents[dim]) if dim == "z" else list(range(extents[dim]))
        found = [dict(one, **{dim: value}) for one in found for value in values]
    return found


def slot_key(slot):
    return (slot["z"], slot["y"], slot["x"])


def route_children(slot, order, extents):
    reached = max([i for i, dim in enumerate(order) if slot[dim] != 0], default=-1)
    found = []
    for i, dim in enumerate(order):
        if i < reached:
            continue
        if dim == "z":
            sides = (1, -1) if i > reached else ((-1,) if slot["z"] > 0 else (1,))
            for side in sides:
                child = dict(slot, z=slot["z"] - side)
                if abs(child["z"]) < extents["z"]:
                    found.append((dim, side, child))
        elif i > reached:
            found.append((dim, 0, dict(slot, **{dim: 1})))
    return found


def route_order(parts, extents):
    chips = [
        (z, y, x) for z in range(extents["z"]) for y in range(extents["y"]) for x in range(extents["x"])
    ]
    free, events, seen = ({}, [], {})
    for chip in chips:
        for part in range(len(parts)):
            events.append((0.0, chip, part, (0, 0, 0)))
    heapq.heapify(events)
    while events:
        now, chip, part, key = heapq.heappop(events)
        seen.setdefault((part, key), []).append(now)
        slot = dict(zip(("z", "y", "x"), key))
        for dim, side, child in route_children(slot, parts[part][2], extents):
            if dim == "z":
                there = (chip[0] + side, chip[1], chip[2])
                if not 0 <= there[0] < extents["z"]:
                    continue
            elif dim == "y":
                there = (chip[0], 1 - chip[1], chip[2])
            else:
                there = (chip[0], chip[1], 1 - chip[2])
            end = max(now, free.get((chip, there), 0.0)) + parts[part][1]
            free[chip, there] = end
            heapq.heappush(events, (end + 22.0, there, part, slot_key(child)))
    return sorted(seen, key=lambda one: (sum(seen[one]) / len(seen[one]), one))


def row_parts(rows):
    first = (rows * 3 // 8) // 16 * 16
    second = (rows * 7 // 16) // 16 * 16
    return [
        (0, first, ("z", "x", "y")),
        (first, second, ("z", "y", "x")),
        (first + second, rows - first - second, ("x", "y", "z")),
    ]


class Place:
    def __init__(self, extents):
        dp, ctx = (lax.axis_index("dp"), lax.axis_index("ctx"))
        self.extents = extents
        self.z, self.core = (dp // 2, dp % 2)
        self.y, self.x = (ctx // 2, ctx % 2)
        self.dp, self.ctx = (dp, ctx)

    def valid(self, slot):
        if slot["z"] == 0:
            return None
        z = self.z + slot["z"]
        return (z >= 0) & (z < self.extents["z"])

    def source(self, slot):
        y = self.y if slot["y"] == 0 else 1 - self.y
        x = self.x if slot["x"] == 0 else 1 - self.x
        return (self.z + slot["z"], y, x)

    def chip_index(self, slot):
        z, y, x = self.source(slot)
        return (z * 2 + y) * 2 + x

    def shard_index(self, slot, core):
        z, y, x = self.source(slot)
        return ((z * 2 + core) * 2 + y) * 2 + x

    def neighbour(self, dim, side):
        if dim == "z":
            return (self.dp + 2 * side, self.ctx)
        if dim == "core":
            return (self.dp + 1 - 2 * self.core, self.ctx)
        if dim == "y":
            return (self.dp, (1 - self.y) * 2 + self.x)
        return (self.dp, self.y * 2 + 1 - self.x)

    def has(self, dim, side):
        if dim != "z":
            return None
        return (self.z + side < self.extents["z"]) if side > 0 else (self.z + side >= 0)

    def greet(self, whole=False):
        barrier = pltpu.get_barrier_semaphore()
        total = 3
        for dim in ("core", "x", "y"):
            pl.semaphore_signal(barrier, 1, device_id=self.neighbour(dim, 0), device_id_type=MESH)
        if whole:
            for z in range(self.extents["z"]):

                @pl.when(self.z != z)
                def _():
                    pl.semaphore_signal(
                        barrier, 1, device_id=(2 * z + self.core, self.ctx), device_id_type=MESH
                    )

            total = total + self.extents["z"] - 1
        else:
            for side in (1, -1):
                near = self.has("z", side)

                @pl.when(near)
                def _():
                    pl.semaphore_signal(
                        barrier, 1, device_id=self.neighbour("z", side), device_id_type=MESH
                    )

                total = total + near.astype(jnp.int32)
        pl.semaphore_wait(barrier, total)


MESH = pl.DeviceIdType.MESH


def both(left, right):
    if left is None:
        return right
    return left if right is None else left & right


def guarded(condition, body):
    if condition is None:
        body()
    else:
        pl.when(condition)(body)


def drain(ref, sem):
    pltpu.make_async_copy(ref, ref, sem).wait()


def gather_kernel(
    extents, parts, order, shard_ref, out_ref, got, side_got, side_sent, flat_sent, z_sent, own_sem
):
    place = Place(extents)
    chips = extents["z"] * extents["y"] * extents["x"]
    rank = {}
    for part, (_, _, dims) in enumerate(parts):
        for slot in route_slots(dims, extents):
            rank[part, slot_key(slot)] = len(rank)
    place.greet()
    mine = place.shard_index({"z": 0, "y": 0, "x": 0}, place.core)
    own = pltpu.make_async_copy(shard_ref, out_ref.at[mine], own_sem)
    own.start()
    waits = []
    for part, key in order:
        start, rows, dims = parts[part]
        slot = dict(zip(("z", "y", "x"), key))
        number = rank[part, key]

        def step(part=part, key=key, start=start, rows=rows, dims=dims, slot=slot, number=number):
            block = out_ref.at[place.shard_index(slot, place.core), pl.ds(start, rows)]
            held = shard_ref.at[pl.ds(start, rows)] if key == (0, 0, 0) else block
            if key != (0, 0, 0):
                drain(block, got.at[number])
            for dim, side, child in route_children(slot, dims, extents):
                there = rank[part, slot_key(child)]
                if dim == "z":
                    sent = z_sent.at[number, (side + 1) // 2]
                else:
                    sent = flat_sent.at[part, 0 if dim == "x" else 1]
                copy = pltpu.make_async_remote_copy(
                    src_ref=held,
                    dst_ref=block,
                    send_sem=sent,
                    recv_sem=got.at[there],
                    device_id=place.neighbour(dim, side),
                    device_id_type=MESH,
                )
                guarded(place.has(dim, side), copy.start)
            pltpu.make_async_remote_copy(
                src_ref=held,
                dst_ref=block,
                send_sem=side_sent,
                recv_sem=side_got,
                device_id=place.neighbour("core", 0),
                device_id_type=MESH,
            ).start()

        guarded(place.valid(slot), step)
        for dim, side, _ in route_children(slot, dims, extents):
            if dim == "z":
                waits.append((slot, side, start, rows, z_sent.at[number, (side + 1) // 2]))
    own.wait()
    drain(out_ref.at[pl.ds(0, chips)], side_got)
    drain(out_ref.at[pl.ds(0, chips)], side_sent)
    for part, (start, rows, dims) in enumerate(parts):
        counts = {"x": 0, "y": 0}
        for slot in route_slots(dims, extents):
            if slot["z"] < 0:
                continue
            for dim, _, _ in route_children(slot, dims, extents):
                if dim != "z":
                    counts[dim] = counts[dim] + 1
        for dim in ("x", "y"):
            drain(
                out_ref.at[pl.ds(0, counts[dim]), pl.ds(start, rows)],
                flat_sent.at[part, 0 if dim == "x" else 1],
            )
    for slot, side, start, rows, sent in waits:
        guarded(
            both(place.valid(slot), place.has("z", side)),
            functools.partial(drain, out_ref.at[0, pl.ds(start, rows)], sent),
        )


def gathered(shard, extents, number):
    rows, columns = shard.shape
    total = 2 * extents["z"] * extents["y"] * extents["x"]
    parts = row_parts(rows)
    order = route_order(parts, extents)
    slots = len(order)
    whole = pl.pallas_call(
        functools.partial(gather_kernel, extents, parts, order),
        out_shape=jax.ShapeDtypeStruct((total, rows, columns), shard.dtype),
        in_specs=[pl.BlockSpec(memory_space=pltpu.VMEM)],
        out_specs=pl.BlockSpec(memory_space=pl.ANY),
        scratch_shapes=[
            pltpu.SemaphoreType.DMA((slots,)),
            pltpu.SemaphoreType.DMA,
            pltpu.SemaphoreType.DMA,
            pltpu.SemaphoreType.DMA((len(parts), 2)),
            pltpu.SemaphoreType.DMA((slots, 2)),
            pltpu.SemaphoreType.DMA,
        ],
        compiler_params=pltpu.CompilerParams(collective_id=number, has_side_effects=True),
    )(shard)
    return whole.reshape(total * rows, columns)


CHILD_SEM = {("z", 1): 0, ("z", -1): 1, ("x", 0): 2, ("y", 0): 3}


def route_parent(slot):
    def up(dims):
        last = max(i for i, dim in enumerate(dims) if slot[dim] != 0)
        dim = dims[last]
        if dim != "z":
            return (dim, 0, 0, dict(slot, **{dim: 0}))
        side = 1 if slot["z"] > 0 else -1
        return (dim, side, -side, dict(slot, z=slot["z"] - side))

    return up


def child_rooms(dims, extents):
    rooms, base = ({}, 0)
    for i, dim in enumerate(dims):
        names = dims[:i] + (("z",) if dim == "z" else ())
        size = 1
        for name in names:
            size = size * extents[name]
        for side in (1, -1) if dim == "z" else (0,):
            rooms[dim, side] = (base, names)
            base = base + size
    return (rooms, base)


def small_steps(place, small_ref, total_ref, room_ref, small_got, small_sent):
    axes = ["core", "x", "y", "z"]
    spot = {"core": place.core, "x": place.x, "y": place.y, "z": place.z}
    count = dict(place.extents, core=2)

    def peer(dim, other):
        if dim == "z":
            return (other * 2 + place.core, place.ctx)
        return place.neighbour(dim, 0)

    def send(level):
        dim = axes[level]
        mine = spot[dim]
        source = small_ref if level == 0 else total_ref.at[level - 1]
        room_ref[level, mine] = source[...]
        for other in range(count[dim]):
            copy = pltpu.make_async_remote_copy(
                src_ref=source,
                dst_ref=room_ref.at[level, mine],
                send_sem=small_sent.at[level, other],
                recv_sem=small_got.at[level, mine],
                device_id=peer(dim, other),
                device_id_type=MESH,
            )
            pl.when(mine != other)(copy.start)

    def finish(level):
        dim = axes[level]
        mine = spot[dim]
        for other in range(count[dim]):
            room = room_ref.at[level, other]
            pl.when(mine != other)(functools.partial(drain, room, small_got.at[level, other]))
        value = room_ref[level, 0]
        for other in range(1, count[dim]):
            value = value + room_ref[level, other]
        total_ref[level] = value
        if level + 1 < len(axes):
            send(level + 1)

    def close():
        for level, dim in enumerate(axes):
            for other in range(count[dim]):
                pl.when(spot[dim] != other)(
                    functools.partial(drain, room_ref.at[level, 0], small_sent.at[level, other])
                )

    return (send, finish, close)


def scatter_kernel(extents, parts, order, small, *refs):
    left_ref, right_ref, refs = (refs[0], refs[1], refs[2:])
    if small:
        small_ref, out_ref, total_ref, refs = (refs[0], refs[1], refs[2], refs[3:])
    else:
        out_ref, refs = (refs[0], refs[1:])
    count = len(parts)
    stages, sides, rooms, accs = [refs[i * count : (i + 1) * count] for i in range(4)]
    side_got, child_got, side_sent, sent = refs[4 * count : 4 * count + 4]
    place = Place(extents)
    chips = extents["z"] * extents["y"] * extents["x"]
    rank = {}
    for part, (_, _, dims) in enumerate(parts):
        for slot in route_slots(dims, extents):
            rank[part, slot_key(slot)] = len(rank)
    place.greet(whole=small)
    if small:
        send, finish, close = small_steps(place, small_ref, total_ref, *refs[4 * count + 4 :])
        send(0)

    def product(slot, part, core):
        start, rows, _ = parts[part]
        return dot(left_ref[place.shard_index(slot, core), pl.ds(start, rows)], right_ref[...])

    def room_index(part, slot, dim, side):
        z, y, x = place.source(slot)
        spot = {"z": z, "y": y, "x": x}
        base, names = child_rooms(parts[part][2], extents)[0][dim, side]
        index = 0
        for name in names:
            index = index * extents[name] + spot[name]
        return base + index

    def hand_over(part, key):
        slot = dict(zip(("z", "y", "x"), key))

        def step():
            chip = place.chip_index(slot)
            stage = stages[part].at[chip]
            stage[...] = product(slot, part, 1 - place.core).astype(jnp.bfloat16)
            pltpu.make_async_remote_copy(
                src_ref=stage,
                dst_ref=sides[part].at[chip],
                send_sem=side_sent.at[part],
                recv_sem=side_got.at[rank[part, key]],
                device_id=place.neighbour("core", 0),
                device_id_type=MESH,
            ).start()

        guarded(place.valid(slot), step)

    def merge(part, key):
        start, rows, dims = parts[part]
        slot = dict(zip(("z", "y", "x"), key))
        number = rank[part, key]

        def step():
            side = sides[part].at[place.chip_index(slot)]
            acc = accs[part]
            acc[...] = product(slot, part, place.core)
            drain(side, side_got.at[number])
            acc[...] += side[...].astype(jnp.float32)
            for dim, sign, _ in route_children(slot, dims, extents):
                room = rooms[part].at[room_index(part, slot, dim, sign)]
                got = child_got.at[number, CHILD_SEM[dim, sign]]

                def take(room=room, got=got):
                    drain(room, got)
                    acc[...] += room[...].astype(jnp.float32)

                guarded(place.has(dim, sign), take)
            if key == (0, 0, 0):
                out_ref[pl.ds(start, rows)] = acc[...]
                return
            side[...] = acc[...].astype(jnp.bfloat16)
            dim, sign, seen, parent = route_parent(slot)(dims)
            pltpu.make_async_remote_copy(
                src_ref=side,
                dst_ref=rooms[part].at[room_index(part, slot, dim, seen)],
                send_sem=sent.at[part],
                recv_sem=child_got.at[rank[part, slot_key(parent)], CHILD_SEM[dim, seen]],
                device_id=place.neighbour(dim, sign),
                device_id_type=MESH,
            ).start()

        guarded(place.valid(slot), step)

    ahead = 8
    for one in order[:ahead]:
        hand_over(*one)
    for i, one in enumerate(order):
        if i + ahead < len(order):
            hand_over(*order[i + ahead])
        merge(*one)
        if small and (i + 1) % (len(order) // 5) == 0 and (i + 1) // (len(order) // 5) <= 4:
            finish((i + 1) // (len(order) // 5) - 1)
    if small:
        close()
    for part in range(count):
        drain(stages[part], side_sent.at[part])
        drain(sides[part].at[pl.ds(0, chips - 1)], sent.at[part])


def scattered(left, right, small, extents, number):
    total, rows, depth = left.shape
    columns = right.shape[1]
    chips = total // 2
    parts = row_parts(rows)
    order = list(reversed(route_order(parts, extents)))
    slots = len(order)
    vmem = pl.BlockSpec(memory_space=pltpu.VMEM)
    args = (left, right)
    outs = [jax.ShapeDtypeStruct((rows, columns), jnp.float32)]
    scratch = (
        [pltpu.VMEM((chips, size, columns), jnp.bfloat16) for _, size, _ in parts]
        + [pltpu.VMEM((chips, size, columns), jnp.bfloat16) for _, size, _ in parts]
        + [
            pltpu.VMEM((child_rooms(dims, extents)[1], size, columns), jnp.bfloat16)
            for _, size, dims in parts
        ]
        + [pltpu.VMEM((size, columns), jnp.float32) for _, size, _ in parts]
        + [
            pltpu.SemaphoreType.DMA((slots,)),
            pltpu.SemaphoreType.DMA((slots, 4)),
            pltpu.SemaphoreType.DMA((len(parts),)),
            pltpu.SemaphoreType.DMA((len(parts),)),
        ]
    )
    if small is not None:
        args = args + (small,)
        outs.append(jax.ShapeDtypeStruct((4,) + small.shape, jnp.float32))
        most = max(2, extents["z"])
        scratch = scratch + [
            pltpu.VMEM((4, most) + small.shape, jnp.float32),
            pltpu.SemaphoreType.DMA((4, most)),
            pltpu.SemaphoreType.DMA((4, most)),
        ]
    return pl.pallas_call(
        functools.partial(scatter_kernel, extents, parts, order, small is not None),
        out_shape=outs,
        in_specs=[vmem] * len(args),
        out_specs=[vmem] * len(outs),
        scratch_shapes=scratch,
        compiler_params=pltpu.CompilerParams(
            collective_id=number, has_side_effects=True, vmem_limit_bytes=56 * 1024 * 1024
        ),
    )(*args)


def routed():
    return lax.axis_size("ctx") == 4 and lax.axis_size("dp") % 2 == 0


def route_extents():
    return {"z": lax.axis_size("dp") // 2, "y": 2, "x": 2}


def all_rows(shard, number):
    if routed():
        return gathered(shard, route_extents(), number)
    return lax.all_gather(shard, ("dp", "ctx"), axis=0, tiled=True)


def owner_sums(first_left, first_right, second_left, second_right, small, number):
    if not routed():
        grad = to_owners(owner_rows(first_left, first_right, second_left, second_right))
        return (grad, None if small is None else lax.psum(small, ("dp", "ctx")))
    tokens = first_left.shape[0]
    left = jnp.concatenate(
        [
            jnp.pad(first_left.T, ((0, 0), (0, tokens))),
            jnp.pad(second_left.T, ((0, 0), (tokens, 0))),
        ]
    )
    devices = lax.axis_size("dp") * lax.axis_size("ctx")
    left = left.reshape(devices, left.shape[0] // devices, 2 * tokens)
    right = jnp.concatenate([first_right, second_right])
    if small is None:
        return (scattered(left, right, None, route_extents(), number)[0], None)
    extent = small.shape[0]
    rows = -(-extent // 1024) * 8
    packed = jnp.pad(small, (0, rows * 128 - extent)).reshape(rows, 128)
    grad, totals = scattered(left, right, packed, route_extents(), number)
    return (grad, totals[3].reshape(-1)[:extent])


def shifted(shard, by):
    return passed_along(shard, "ctx", by)


def per_device(
    inputs,
    segments,
    cotangent,
    mixer_params,
    mixer_first,
    mixer_second,
    feed_params,
    feed_first,
    feed_second,
    small_params,
    small_first,
    small_second,
):
    mixer_weights = all_rows(mixer_params.astype(jnp.bfloat16), 0)
    feed_half, mixer_weights = lax.optimization_barrier(
        (feed_params.astype(jnp.bfloat16), mixer_weights)
    )
    feed_weights = all_rows(feed_half, 1)
    conv_weight, gain_first, gain_second, out_gain, gate_rows, decay_log, decay_bias = unpack_small(
        small_params
    )
    channels = 2 * H * DK + H * DV
    input_rows = channels + H * DV
    margin = CONV - 1
    in_weight = mixer_weights[:input_rows]
    out_weight = mixer_weights[input_rows:]
    up_weight = feed_weights[: 2 * FF]
    down_weight = feed_weights[2 * FF :]
    tokens_here = inputs[0]
    cotangent_here = cotangent[0]
    token_count = tokens_here.shape[0]
    position = lax.axis_index("ctx") * token_count
    segment_padded = jnp.concatenate([jnp.full((margin,), -1, jnp.int32), segments[0]])
    segment_wide = lax.dynamic_slice_in_dim(segment_padded, position, token_count + margin)
    segment_ids = segment_wide[margin:]
    segment_before = segment_wide[margin - 1]
    inverse_first = lax.rsqrt(
        jnp.mean(tokens_here * tokens_here, axis=-1, keepdims=True) + EPS_NORM
    )
    normed = (tokens_here * inverse_first * gain_first).astype(jnp.bfloat16)
    gate_half = gate_rows.astype(jnp.bfloat16)
    logits = jnp.einsum("td,rd->tr", normed, gate_half, preferred_element_type=jnp.float32)
    rim_normed = shifted(normed[token_count - margin :], 1)
    projected = jnp.einsum("td,rd->tr", normed, in_weight, preferred_element_type=jnp.float32)
    rim_rows = jnp.einsum(
        "td,rd->tr", rim_normed, in_weight[:channels], preferred_element_type=jnp.float32
    ).astype(jnp.bfloat16)
    conv_input = projected[:, :channels].astype(jnp.bfloat16)
    gate_pre = projected[:, channels:]
    extended = jnp.concatenate([rim_rows, conv_input]).astype(jnp.float32)

    active, active_back = jax.vjp(
        lambda wide, taps: active_rows(wide, taps, segment_wide), extended, conv_weight
    )
    span = min(SPAN, token_count)
    count = token_count // span
    scalars, scalars_back = jax.vjp(
        lambda *args: block_scalars(*args, segment_ids, segment_before, span),
        logits[:, :H],
        logits[:, H:],
        decay_log,
        decay_bias,
    )
    beta, running, carried, last = scalars
    segment_rows = jnp.broadcast_to(
        segment_ids.astype(jnp.float32).reshape(1, count, span), beta.shape
    )
    blank = jnp.zeros_like(beta)
    row_pack = jnp.stack(
        [beta, running, segment_rows, carried, last, blank, blank, blank], axis=2
    )
    column_pack = jnp.swapaxes(row_pack, 2, 3)
    groups = H // GROUP
    key_blocks = H * DK // (GROUP * DK)
    value_start = 2 * H * DK // (GROUP * DV)
    query_spec = pl.BlockSpec((span, GROUP * DK), lambda c, g: (c, g))
    key_spec = pl.BlockSpec((span, GROUP * DK), lambda c, g: (c, g + key_blocks))
    value_spec = pl.BlockSpec((span, GROUP * DV), lambda c, g: (c, g + value_start))
    wide_spec = pl.BlockSpec((span, GROUP * DV), lambda c, g: (c, g))
    row_spec = pl.BlockSpec((GROUP, 1, 8, span), lambda c, g: (g, c, 0, 0))
    column_spec = pl.BlockSpec((GROUP, 1, span, 8), lambda c, g: (g, c, 0, 0))
    inverse_spec = pl.BlockSpec((1, GROUP, span, span), lambda c, g: (c, g, 0, 0))
    square_spec = pl.BlockSpec((1, GROUP, DK, DK), lambda c, g: (c, g, 0, 0))
    state_spec = pl.BlockSpec((1, GROUP, DK, DV), lambda c, g: (c, g, 0, 0))
    gain_spec = pl.BlockSpec((1, DV), lambda c, g: (0, 0))
    key_out = ((token_count, H * DK), jnp.float32)
    value_out = ((token_count, H * DV), jnp.float32)
    state_out = ((count, H, DK, DV), jnp.float32)
    grid = (count, groups)
    inverse, w_part, u_part, r_part, o_part, transfers, offsets = kernel_call(
        block_kernel,
        grid,
        (active, active, active, row_pack, column_pack),
        [query_spec, key_spec, value_spec, row_spec, column_spec],
        [
            ((count, H, span, span), jnp.float32),
            key_out,
            value_out,
            key_out,
            value_out,
            ((count, H, DK, DK), jnp.float32),
            state_out,
        ],
        [inverse_spec, query_spec, wide_spec, query_spec, wide_spec, square_spec, state_spec],
    )

    def advance(left, right):
        return jnp.einsum(
            "hij,hjw->hiw", left, right, precision=CORE, preferred_element_type=jnp.float32
        )

    def advance_back(left, right):
        return jnp.einsum(
            "hji,hjw->hiw", left, right, precision=CORE, preferred_element_type=jnp.float32
        )

    transfer, offset_state = (transfers[0], offsets[0])
    for block in range(1, count):
        transfer = advance(transfers[block], transfer)
        offset_state = advance(transfers[block], offset_state) + offsets[block]
    ring = lax.axis_size("ctx")
    transfer_half = transfer.astype(jnp.bfloat16)
    offset_half = offset_state.astype(jnp.bfloat16)
    befores = [
        (shifted(transfer_half, by), shifted(offset_half, by)) for by in range(1, ring)
    ]
    state_in = jnp.zeros((H, DK, DV), jnp.float32)
    for transfer_there, offset_there in reversed(befores):
        state_in = advance(transfer_there.astype(jnp.float32), state_in) + offset_there
    states = [state_in]
    for block in range(count - 1):
        states.append(advance(transfers[block], states[-1]) + offsets[block])
    states = jnp.stack(states)
    gain_row = out_gain.reshape(1, DV)
    recurrent_out, mix_half = kernel_call(
        output_kernel,
        grid,
        (r_part, o_part, states, gate_pre, gain_row),
        [query_spec, wide_spec, state_spec, wide_spec, gain_spec],
        [value_out, ((token_count, H * DV), jnp.bfloat16)],
        [wide_spec, wide_spec],
    )
    afters = [shifted(transfer_half, -by) for by in range(1, ring)]
    hidden = tokens_here + jnp.dot(mix_half, out_weight, preferred_element_type=jnp.float32)
    inverse_second = lax.rsqrt(jnp.mean(hidden * hidden, axis=-1, keepdims=True) + EPS_NORM)
    hidden_normed = (hidden * inverse_second * gain_second).astype(jnp.bfloat16)
    gate_up = jnp.einsum("td,rd->tr", hidden_normed, up_weight, preferred_element_type=jnp.float32)
    gate_part = gate_up[:, :FF]
    up_part = gate_up[:, FF:]
    middle = (jax.nn.silu(gate_part) * up_part).astype(jnp.bfloat16)
    result = hidden + jnp.dot(middle, down_weight, preferred_element_type=jnp.float32)
    cotangent_half = cotangent_here.astype(jnp.bfloat16)
    grad_middle = jnp.einsum(
        "td,fd->tf", cotangent_half, down_weight, preferred_element_type=jnp.float32
    )
    sigmoid_gate = jax.nn.sigmoid(gate_part)
    grad_gate = (
        grad_middle * up_part * (sigmoid_gate + gate_part * sigmoid_gate * (1.0 - sigmoid_gate))
    )
    grad_up = grad_middle * gate_part * sigmoid_gate
    grad_gate_up = jnp.concatenate([grad_gate, grad_up], axis=1).astype(jnp.bfloat16)
    grad_hidden_normed = jnp.dot(grad_gate_up, up_weight, preferred_element_type=jnp.float32)
    grad_hidden = cotangent_here + norm_back(
        hidden, inverse_second, gain_second, grad_hidden_normed
    )
    grad_gain_second = jnp.sum(grad_hidden_normed * hidden * inverse_second, axis=0)
    grad_hidden_half = grad_hidden.astype(jnp.bfloat16)
    feed_grad, _ = owner_sums(grad_gate_up, hidden_normed, middle, cotangent_half, None, 2)
    grad_mix = jnp.einsum(
        "td,rd->tr", grad_hidden_half, out_weight, preferred_element_type=jnp.float32
    )
    partial_spec = pl.BlockSpec((1, 1, DV), lambda c, g: (c * groups + g, 0, 0))
    grad_recurrent, grad_gate_pre, gain_parts, locals_back = kernel_call(
        gate_back_kernel,
        grid,
        (grad_mix, recurrent_out, gate_pre, gain_row, r_part),
        [wide_spec, wide_spec, wide_spec, gain_spec, query_spec],
        [value_out, value_out, ((count * groups, 1, DV), jnp.float32), state_out],
        [wide_spec, wide_spec, partial_spec, state_spec],
    )
    grad_out_gain = jnp.sum(gain_parts, axis=(0, 1))
    local_part = locals_back[count - 1]
    for block in range(count - 2, -1, -1):
        local_part = advance_back(transfers[block], local_part) + locals_back[block]
    local_half = local_part.astype(jnp.bfloat16)
    local_afters = [shifted(local_half, -by) for by in range(1, ring)]
    state_grad = jnp.zeros((H, DK, DV), jnp.float32)
    for transfer_there, local_there in reversed(list(zip(afters, local_afters))):
        state_grad = advance_back(transfer_there.astype(jnp.float32), state_grad) + local_there
    nexts = [state_grad]
    for block in range(count - 1, 0, -1):
        nexts.append(advance_back(transfers[block], nexts[-1]) + locals_back[block])
    nexts = jnp.stack(nexts[::-1])
    grad_q, grad_k, grad_v, grad_row_pack, grad_column_pack = kernel_call(
        block_back_kernel,
        grid,
        (
            active,
            active,
            active,
            row_pack,
            column_pack,
            inverse,
            w_part,
            u_part,
            states,
            grad_recurrent,
            nexts,
        ),
        [
            query_spec,
            key_spec,
            value_spec,
            row_spec,
            column_spec,
            inverse_spec,
            query_spec,
            wide_spec,
            state_spec,
            wide_spec,
            state_spec,
        ],
        [key_out, key_out, value_out, (row_pack.shape, jnp.float32), (column_pack.shape, jnp.float32)],
        [query_spec, query_spec, wide_spec, row_spec, column_spec],
    )
    grad_pack = grad_row_pack + jnp.swapaxes(grad_column_pack, 2, 3)
    grad_beta_logit, grad_alpha_logit, grad_decay_log, grad_decay_bias = scalars_back(
        (grad_pack[:, :, 0], grad_pack[:, :, 1], grad_pack[:, :, 3], grad_pack[:, :, 4])
    )
    grad_wide, grad_conv = active_back(jnp.concatenate([grad_q, grad_k, grad_v], axis=1))
    back_rim = passed_along(grad_wide[:margin].astype(jnp.bfloat16), "ctx", -1).astype(jnp.float32)
    grad_conv_input = grad_wide[margin:]
    grad_conv_input = jnp.concatenate(
        [
            grad_conv_input[: token_count - margin],
            grad_conv_input[token_count - margin :] + back_rim,
        ]
    )
    grad_projected = jnp.concatenate([grad_conv_input, grad_gate_pre], axis=1).astype(jnp.bfloat16)
    grad_logits = jnp.concatenate([grad_beta_logit, grad_alpha_logit], axis=1).astype(jnp.bfloat16)
    grad_normed = jnp.dot(grad_projected, in_weight, preferred_element_type=jnp.float32)
    grad_normed = grad_normed + jnp.dot(grad_logits, gate_half, preferred_element_type=jnp.float32)
    grad_inputs = grad_hidden + norm_back(tokens_here, inverse_first, gain_first, grad_normed)
    grad_gain_first = jnp.sum(grad_normed * tokens_here * inverse_first, axis=0)
    gate_grad = jnp.einsum("tr,td->rd", grad_logits, normed, preferred_element_type=jnp.float32)
    small_local = jnp.concatenate(
        [
            grad_conv.reshape(-1),
            grad_gain_first,
            grad_gain_second,
            grad_out_gain,
            gate_grad.reshape(-1),
            grad_decay_log,
            grad_decay_bias,
        ]
    )
    mixer_grad, small_grad = owner_sums(
        grad_projected, normed, mix_half, grad_hidden_half, small_local, 3
    )
    mixer_new, mixer_moment, mixer_square = adamw(
        mixer_params, mixer_grad, mixer_first, mixer_second
    )
    feed_new, feed_moment, feed_square = adamw(feed_params, feed_grad, feed_first, feed_second)
    small_new, small_moment, small_square = adamw(
        small_params, small_grad, small_first, small_second
    )
    return (
        result[None],
        grad_inputs[None],
        mixer_grad,
        feed_grad,
        small_grad,
        mixer_new,
        mixer_moment,
        mixer_square,
        feed_new,
        feed_moment,
        feed_square,
        small_new,
        small_moment,
        small_square,
    )


def solution(mesh):
    in_specs = (
        P("dp", "ctx", None),
        P("dp", None),
        P("dp", "ctx", None),
        P(("dp", "ctx"), None),
        P(("dp", "ctx"), None),
        P(("dp", "ctx"), None),
        P(("dp", "ctx"), None),
        P(("dp", "ctx"), None),
        P(("dp", "ctx"), None),
        P(),
        P(),
        P(),
    )
    out_specs = (
        P("dp", "ctx", None),
        P("dp", "ctx", None),
        P(("dp", "ctx"), None),
        P(("dp", "ctx"), None),
        P(),
        P(("dp", "ctx"), None),
        P(("dp", "ctx"), None),
        P(("dp", "ctx"), None),
        P(("dp", "ctx"), None),
        P(("dp", "ctx"), None),
        P(("dp", "ctx"), None),
        P(),
        P(),
        P(),
    )
    return jax.shard_map(
        per_device, mesh=mesh, in_specs=in_specs, out_specs=out_specs, check_vma=False
    )
```

```python
import functools
import heapq

import jax
import jax.numpy as jnp
from jax import lax
from jax.experimental import pallas as pl
from jax.experimental.pallas import tpu as pltpu
from jax.sharding import PartitionSpec as P

D = 1024
H = 8
DK = 128
DV = 256
FF = 2816
CONV = 4
SPAN = 128
GROUP = 4
STEP = 10


PRECISE = lax.Precision.HIGHEST
CORE = lax.Precision.DEFAULT
EPS_NORM = 1e-06
EPS_GATE = 1e-05
EPS_KEYS = 1e-06
LEARN_RATE = 0.002
FIRST_RATE = 0.9
SECOND_RATE = 0.95
EPS_ADAM = 1e-08
WEIGHT_DECAY = 0.1


def passed_along(shard, axis, by):
    count = lax.axis_size(axis)
    pairs = [(i, i + by) for i in range(count) if 0 <= i + by < count]
    return lax.ppermute(shard, axis, pairs)


def dot(left, right, contract=((1,), (0,)), precision=None):
    return lax.dot_general(
        left, right, (contract, ((), ())), precision=precision, preferred_element_type=jnp.float32
    )


def unit_rows(raw, scale):
    inverse = lax.rsqrt(jnp.sum(raw * raw, axis=-1, keepdims=True) + EPS_KEYS)
    return (raw * (inverse * scale), inverse)


def unit_back(raw, inverse, scale, upstream):
    upstream = upstream * scale
    shared = jnp.sum(raw * upstream, axis=-1, keepdims=True)
    return inverse * upstream - raw * (inverse * inverse * inverse * shared)


def block_decays(rows, columns, extent):
    places = lax.broadcasted_iota(jnp.int32, (extent, extent), 0)
    others = lax.broadcasted_iota(jnp.int32, (extent, extent), 1)
    keep = (columns[:, 2:3] == rows[2:3, :]) & (places >= others)
    spread = jnp.minimum(columns[:, 1:2] - rows[1:2, :], 0.0)
    return (jnp.where(keep, jnp.exp(spread), 0.0), places, others)


def block_kernel(
    q_ref, k_ref, v_ref, row_ref, column_ref,
    inverse_ref, w_ref, u_ref, r_ref, o_ref, transfer_ref, offset_ref,
):
    group = row_ref.shape[0]
    extent = q_ref.shape[0]
    systems, solved, pieces = ([], [], [])
    for h in range(group):
        rows, columns = (row_ref[h, 0], column_ref[h, 0])
        keys = slice(h * DK, (h + 1) * DK)
        queries, _ = unit_rows(q_ref[:, keys], DK ** (-0.5))
        key_rows, _ = unit_rows(k_ref[:, keys], 1.0)
        decays, places, others = block_decays(rows, columns, extent)
        weighted = decays * rows[0:1, :]
        key_key = dot(key_rows, key_rows, ((1,), (1,)), CORE)
        system = jnp.where(places > others, weighted * key_key, 0.0)
        apart = places ^ others
        systems.append(system)
        solved.append(
            jnp.where(places == others, 1.0, 0.0) - jnp.where(apart < 2, system, 0.0)
        )
        mixing = weighted * dot(queries, key_rows, ((1,), (1,)), CORE)
        pieces.append((queries, key_rows, mixing, columns))
    size = 2
    while size < extent:
        level = (apart >= size) & (apart < 2 * size)
        halves = [
            dot(solved[h], jnp.where(level, systems[h], 0.0), precision=PRECISE)
            for h in range(group)
        ]
        solved = [
            solved[h] - dot(halves[h], solved[h], precision=PRECISE) for h in range(group)
        ]
        size = 2 * size
    for h in range(group):
        queries, key_rows, mixing, columns = pieces[h]
        keys = slice(h * DK, (h + 1) * DK)
        values = slice(h * DV, (h + 1) * DV)
        carried = columns[:, 3:4]
        inverse_ref[0, h] = solved[h]
        w_part = dot(solved[h], carried * key_rows, precision=CORE)
        u_part = dot(solved[h], v_ref[:, values], precision=CORE)
        w_ref[:, keys] = w_part
        u_ref[:, values] = u_part
        r_ref[:, keys] = carried * queries - dot(mixing, w_part, precision=CORE)
        o_ref[:, values] = dot(mixing, u_part, precision=CORE)
        last_keys = key_rows * columns[:, 4:5]
        rank = lax.broadcasted_iota(jnp.int32, (DK, DK), 0)
        file = lax.broadcasted_iota(jnp.int32, (DK, DK), 1)
        transfer_ref[0, h] = jnp.where(
            rank == file, carried[extent - 1 : extent, :], 0.0
        ) - dot(last_keys, w_part, ((0,), (0,)), CORE)
        offset_ref[0, h] = dot(last_keys, u_part, ((0,), (0,)), CORE)


def output_kernel(r_ref, o_ref, state_ref, gate_ref, gain_ref, recurrent_ref, mix_ref):
    for h in range(state_ref.shape[1]):
        keys = slice(h * DK, (h + 1) * DK)
        values = slice(h * DV, (h + 1) * DV)
        recurrent = o_ref[:, values] + dot(r_ref[:, keys], state_ref[0, h], precision=CORE)
        recurrent_ref[:, values] = recurrent
        inverse = lax.rsqrt(jnp.mean(recurrent * recurrent, axis=-1, keepdims=True) + EPS_GATE)
        mix_ref[:, values] = (
            recurrent * inverse * gain_ref[...] * jax.nn.silu(gate_ref[:, values])
        ).astype(jnp.bfloat16)


def gate_back_kernel(
    mix_ref, recurrent_ref, gate_ref, gain_ref, r_ref,
    grad_ref, grad_gate_ref, grad_gain_ref, local_ref,
):
    total = jnp.zeros((1, DV), jnp.float32)
    for h in range(local_ref.shape[1]):
        keys = slice(h * DK, (h + 1) * DK)
        values = slice(h * DV, (h + 1) * DV)
        upstream, recurrent, gate = (mix_ref[:, values], recurrent_ref[:, values], gate_ref[:, values])
        inverse = lax.rsqrt(jnp.mean(recurrent * recurrent, axis=-1, keepdims=True) + EPS_GATE)
        normal = recurrent * inverse
        sig = jax.nn.sigmoid(gate)
        gain = gain_ref[...]
        grad_gate_ref[:, values] = upstream * normal * gain * (sig + gate * sig * (1.0 - sig))
        scaled = upstream * (gate * sig)
        total = total + jnp.sum(scaled * normal, axis=0, keepdims=True)
        scaled = scaled * gain
        grad = inverse * (scaled - normal * jnp.mean(scaled * normal, axis=-1, keepdims=True))
        grad_ref[:, values] = grad
        local_ref[0, h] = dot(r_ref[:, keys], grad, ((0,), (0,)), CORE)
    grad_gain_ref[0] = total


def block_back_kernel(
    q_ref, k_ref, v_ref, row_ref, column_ref, inverse_ref, w_ref, u_ref, state_ref, grad_ref, next_ref,
    grad_q_ref, grad_k_ref, grad_v_ref, grad_row_ref, grad_column_ref,
):
    group = row_ref.shape[0]
    extent = q_ref.shape[0]
    for h in range(group):
        rows, columns = (row_ref[h, 0], column_ref[h, 0])
        keys = slice(h * DK, (h + 1) * DK)
        values = slice(h * DV, (h + 1) * DV)
        raw_q, raw_k = (q_ref[:, keys], k_ref[:, keys])
        queries, inverse_q = unit_rows(raw_q, DK ** (-0.5))
        key_rows, inverse_k = unit_rows(raw_k, 1.0)
        decays, places, others = block_decays(rows, columns, extent)
        beta = rows[0:1, :]
        carried, last = (columns[:, 3:4], columns[:, 4:5])
        weighted = decays * beta
        strict = places > others
        key_key = dot(key_rows, key_rows, ((1,), (1,)), CORE)
        query_key = dot(queries, key_rows, ((1,), (1,)), CORE)
        state, upstream, after = (state_ref[0, h], grad_ref[:, values], next_ref[0, h])
        delta = u_ref[:, values] - dot(w_ref[:, keys], state, precision=CORE)
        grad_delta = dot(weighted * query_key, upstream, ((0,), (0,)), CORE) + dot(
            key_rows * last, after, precision=CORE
        )
        grad_mixing = dot(upstream, delta, ((1,), (1,)), CORE)
        grad_target = dot(inverse_ref[0, h], grad_delta, ((0,), (0,)), CORE)
        grad_system = jnp.where(strict, -dot(grad_target, delta, ((1,), (1,)), CORE), 0.0)
        up_state = dot(upstream, state, ((1,), (1,)), CORE)
        down_state = dot(grad_target, state, ((1,), (1,)), CORE)
        grad_last = dot(delta, after, ((1,), (1,)), CORE)
        grad_carried = jnp.sum(up_state * queries - down_state * key_rows, axis=-1, keepdims=True)
        line = lax.broadcasted_iota(jnp.int32, (extent, 1), 0)
        grad_carried = grad_carried + jnp.where(
            line == extent - 1, jnp.sum(after * state, keepdims=True), 0.0
        )
        grad_qk = grad_mixing * weighted
        grad_kk = grad_system * weighted
        grad_queries = carried * up_state + dot(grad_qk, key_rows, precision=CORE)
        grad_keys = (
            grad_last * last
            - carried * down_state
            + dot(grad_qk, queries, ((0,), (0,)), CORE)
            + dot(grad_kk, key_rows, precision=CORE)
            + dot(grad_kk, key_rows, ((0,), (0,)), CORE)
        )
        grad_q_ref[:, keys] = unit_back(raw_q, inverse_q, DK ** (-0.5), grad_queries)
        grad_k_ref[:, keys] = unit_back(raw_k, inverse_k, 1.0, grad_keys)
        grad_v_ref[:, values] = grad_target
        spread = (grad_system * key_key + grad_mixing * query_key) * decays
        grad_row_ref[h, 0] = jnp.zeros_like(rows)
        grad_row_ref[h, 0, 0:1, :] = jnp.sum(spread, axis=0, keepdims=True)
        grad_row_ref[h, 0, 1:2, :] = -jnp.sum(spread * beta, axis=0, keepdims=True)
        place = lax.broadcasted_iota(jnp.int32, (extent, 8), 1)
        grad_column_ref[h, 0] = jnp.where(
            place == 1,
            jnp.sum(spread * beta, axis=-1, keepdims=True),
            jnp.where(
                place == 3,
                grad_carried,
                jnp.where(
                    place == 4, jnp.sum(grad_last * key_rows, axis=-1, keepdims=True), 0.0
                ),
            ),
        )


def block_scalars(beta_logit, alpha_logit, decay_log, decay_bias, segment_ids, segment_before, span):
    token_count = beta_logit.shape[0]
    count = token_count // span
    beta = jax.nn.sigmoid(beta_logit)
    log_decay = -jnp.exp(decay_log) * jax.nn.softplus(alpha_logit + decay_bias)

    def blocks(tensor):
        return tensor.T.reshape(H, count, span)

    beta, log_decay = (blocks(beta), blocks(log_decay))
    segment_blocks = segment_ids.reshape(count, span)
    befores = jnp.concatenate([jnp.reshape(segment_before, (1,)), segment_blocks[:-1, -1]])
    upper = (jnp.arange(span)[:, None] <= jnp.arange(span)[None, :]).astype(jnp.float32)
    running = jnp.einsum("hcs,st->hct", log_decay, upper, precision=PRECISE)
    carried = jnp.where((segment_blocks == befores[:, None])[None], jnp.exp(running), 0.0)
    ending = (segment_blocks == segment_blocks[:, -1:])[None]
    last = jnp.where(ending, jnp.exp(jnp.minimum(running[:, :, -1:] - running, 0.0)), 0.0) * beta
    return (beta, running, carried, last)


def kernel_call(body, grid, args, in_specs, outs, out_specs):
    return pl.pallas_call(
        body,
        grid=grid,
        in_specs=in_specs,
        out_specs=out_specs,
        out_shape=[jax.ShapeDtypeStruct(shape, dtype) for shape, dtype in outs],
        compiler_params=pltpu.CompilerParams(vmem_limit_bytes=48 * 1024 * 1024),
    )(*args)


def active_rows(extended, conv_weight, segment_wide):
    margin = CONV - 1
    token_count = extended.shape[0] - margin
    segment_ids = segment_wide[margin:]
    mixed = jnp.zeros((token_count, extended.shape[1]), extended.dtype)
    for offset in range(CONV):
        start_row = margin - offset
        window = extended[start_row : start_row + token_count]
        keep_mask = (segment_wide[start_row : start_row + token_count] == segment_ids)[:, None]
        mixed = mixed + jnp.where(keep_mask, window * conv_weight[offset], 0.0)
    return jax.nn.silu(mixed)


def norm_back(values, inverse, gain_row, upstream):
    weighted = gain_row * upstream
    return inverse * weighted - values * inverse**3 * jnp.mean(
        weighted * values, axis=-1, keepdims=True
    )


def unpack_small(packed):
    channels = 2 * H * DK + H * DV
    bounds = [CONV * channels, D, D, DV, 2 * H * D, H, H]
    pieces = []
    cursor = 0
    for extent in bounds:
        pieces.append(packed[cursor : cursor + extent])
        cursor = cursor + extent
    return (
        pieces[0].reshape(CONV, channels),
        pieces[1],
        pieces[2],
        pieces[3],
        pieces[4].reshape(2 * H, D),
        pieces[5],
        pieces[6],
    )


def adamw(current, gradient, moment, square):
    moment = FIRST_RATE * moment + (1.0 - FIRST_RATE) * gradient
    square = SECOND_RATE * square + (1.0 - SECOND_RATE) * gradient * gradient
    update = (
        moment
        / (1.0 - FIRST_RATE**STEP)
        / (jnp.sqrt(square / (1.0 - SECOND_RATE**STEP)) + EPS_ADAM)
    )
    return (current - LEARN_RATE * (update + WEIGHT_DECAY * current), moment, square)


def owner_rows(first_left, first_right, second_left, second_right):
    def product(left_part, right_part):
        return jnp.einsum(
            "tr,td->rd", left_part, right_part, preferred_element_type=jnp.float32
        ).astype(jnp.bfloat16)

    return jnp.concatenate(
        [product(first_left, first_right), product(second_left, second_right)], axis=0
    )


def to_owners(rows):
    return lax.psum_scatter(rows, ("dp", "ctx"), scatter_dimension=0, tiled=True).astype(
        jnp.float32
    )


def ranks_of(extent):
    return [0] + [side * step for step in range(1, extent) for side in (1, -1)]


def route_slots(order, extents):
    found = [{}]
    for dim in order:
        values = ranks_of(extents[dim]) if dim == "z" else list(range(extents[dim]))
        found = [dict(one, **{dim: value}) for one in found for value in values]
    return found


def slot_key(slot):
    return (slot["z"], slot["y"], slot["x"])


def route_children(slot, order, extents):
    reached = max([i for i, dim in enumerate(order) if slot[dim] != 0], default=-1)
    found = []
    for i, dim in enumerate(order):
        if i < reached:
            continue
        if dim == "z":
            sides = (1, -1) if i > reached else ((-1,) if slot["z"] > 0 else (1,))
            for side in sides:
                child = dict(slot, z=slot["z"] - side)
                if abs(child["z"]) < extents["z"]:
                    found.append((dim, side, child))
        elif i > reached:
            found.append((dim, 0, dict(slot, **{dim: 1})))
    return found


def route_order(parts, extents):
    chips = [
        (z, y, x) for z in range(extents["z"]) for y in range(extents["y"]) for x in range(extents["x"])
    ]
    free, events, seen = ({}, [], {})
    for chip in chips:
        for part in range(len(parts)):
            events.append((0.0, chip, part, (0, 0, 0)))
    heapq.heapify(events)
    while events:
        now, chip, part, key = heapq.heappop(events)
        seen.setdefault((part, key), []).append(now)
        slot = dict(zip(("z", "y", "x"), key))
        for dim, side, child in route_children(slot, parts[part][2], extents):
            if dim == "z":
                there = (chip[0] + side, chip[1], chip[2])
                if not 0 <= there[0] < extents["z"]:
                    continue
            elif dim == "y":
                there = (chip[0], 1 - chip[1], chip[2])
            else:
                there = (chip[0], chip[1], 1 - chip[2])
            end = max(now, free.get((chip, there), 0.0)) + parts[part][1]
            free[chip, there] = end
            heapq.heappush(events, (end + 22.0, there, part, slot_key(child)))
    return sorted(seen, key=lambda one: (sum(seen[one]) / len(seen[one]), one))


def row_parts(rows):
    first = (rows * 3 // 8) // 16 * 16
    second = (rows * 7 // 16) // 16 * 16
    return [
        (0, first, ("z", "x", "y")),
        (first, second, ("z", "y", "x")),
        (first + second, rows - first - second, ("x", "y", "z")),
    ]


class Place:
    def __init__(self, extents):
        dp, ctx = (lax.axis_index("dp"), lax.axis_index("ctx"))
        self.extents = extents
        self.z, self.core = (dp // 2, dp % 2)
        self.y, self.x = (ctx // 2, ctx % 2)
        self.dp, self.ctx = (dp, ctx)

    def valid(self, slot):
        if slot["z"] == 0:
            return None
        z = self.z + slot["z"]
        return (z >= 0) & (z < self.extents["z"])

    def source(self, slot):
        y = self.y if slot["y"] == 0 else 1 - self.y
        x = self.x if slot["x"] == 0 else 1 - self.x
        return (self.z + slot["z"], y, x)

    def chip_index(self, slot):
        z, y, x = self.source(slot)
        return (z * 2 + y) * 2 + x

    def shard_index(self, slot, core):
        z, y, x = self.source(slot)
        return ((z * 2 + core) * 2 + y) * 2 + x

    def neighbour(self, dim, side):
        if dim == "z":
            return (self.dp + 2 * side, self.ctx)
        if dim == "core":
            return (self.dp + 1 - 2 * self.core, self.ctx)
        if dim == "y":
            return (self.dp, (1 - self.y) * 2 + self.x)
        return (self.dp, self.y * 2 + 1 - self.x)

    def has(self, dim, side):
        if dim != "z":
            return None
        return (self.z + side < self.extents["z"]) if side > 0 else (self.z + side >= 0)

    def greet(self, whole=False):
        barrier = pltpu.get_barrier_semaphore()
        total = 3
        for dim in ("core", "x", "y"):
            pl.semaphore_signal(barrier, 1, device_id=self.neighbour(dim, 0), device_id_type=MESH)
        if whole:
            for z in range(self.extents["z"]):

                @pl.when(self.z != z)
                def _():
                    pl.semaphore_signal(
                        barrier, 1, device_id=(2 * z + self.core, self.ctx), device_id_type=MESH
                    )

            total = total + self.extents["z"] - 1
        else:
            for side in (1, -1):
                near = self.has("z", side)

                @pl.when(near)
                def _():
                    pl.semaphore_signal(
                        barrier, 1, device_id=self.neighbour("z", side), device_id_type=MESH
                    )

                total = total + near.astype(jnp.int32)
        pl.semaphore_wait(barrier, total)


MESH = pl.DeviceIdType.MESH


def both(left, right):
    if left is None:
        return right
    return left if right is None else left & right


def guarded(condition, body):
    if condition is None:
        body()
    else:
        pl.when(condition)(body)


def drain(ref, sem):
    pltpu.make_async_copy(ref, ref, sem).wait()


def gather_kernel(
    extents, parts, order, shard_ref, out_ref, got, side_got, side_sent, flat_sent, z_sent, own_sem
):
    place = Place(extents)
    chips = extents["z"] * extents["y"] * extents["x"]
    rank = {}
    for part, (_, _, dims) in enumerate(parts):
        for slot in route_slots(dims, extents):
            rank[part, slot_key(slot)] = len(rank)
    place.greet()
    mine = place.shard_index({"z": 0, "y": 0, "x": 0}, place.core)
    own = pltpu.make_async_copy(shard_ref, out_ref.at[mine], own_sem)
    own.start()
    waits = []
    for part, key in order:
        start, rows, dims = parts[part]
        slot = dict(zip(("z", "y", "x"), key))
        number = rank[part, key]

        def step(part=part, key=key, start=start, rows=rows, dims=dims, slot=slot, number=number):
            block = out_ref.at[place.shard_index(slot, place.core), pl.ds(start, rows)]
            held = shard_ref.at[pl.ds(start, rows)] if key == (0, 0, 0) else block
            if key != (0, 0, 0):
                drain(block, got.at[number])
            for dim, side, child in route_children(slot, dims, extents):
                there = rank[part, slot_key(child)]
                if dim == "z":
                    sent = z_sent.at[number, (side + 1) // 2]
                else:
                    sent = flat_sent.at[part, 0 if dim == "x" else 1]
                copy = pltpu.make_async_remote_copy(
                    src_ref=held,
                    dst_ref=block,
                    send_sem=sent,
                    recv_sem=got.at[there],
                    device_id=place.neighbour(dim, side),
                    device_id_type=MESH,
                )
                guarded(place.has(dim, side), copy.start)
            pltpu.make_async_remote_copy(
                src_ref=held,
                dst_ref=block,
                send_sem=side_sent,
                recv_sem=side_got,
                device_id=place.neighbour("core", 0),
                device_id_type=MESH,
            ).start()

        guarded(place.valid(slot), step)
        for dim, side, _ in route_children(slot, dims, extents):
            if dim == "z":
                waits.append((slot, side, start, rows, z_sent.at[number, (side + 1) // 2]))
    own.wait()
    drain(out_ref.at[pl.ds(0, chips)], side_got)
    drain(out_ref.at[pl.ds(0, chips)], side_sent)
    for part, (start, rows, dims) in enumerate(parts):
        counts = {"x": 0, "y": 0}
        for slot in route_slots(dims, extents):
            if slot["z"] < 0:
                continue
            for dim, _, _ in route_children(slot, dims, extents):
                if dim != "z":
                    counts[dim] = counts[dim] + 1
        for dim in ("x", "y"):
            drain(
                out_ref.at[pl.ds(0, counts[dim]), pl.ds(start, rows)],
                flat_sent.at[part, 0 if dim == "x" else 1],
            )
    for slot, side, start, rows, sent in waits:
        guarded(
            both(place.valid(slot), place.has("z", side)),
            functools.partial(drain, out_ref.at[0, pl.ds(start, rows)], sent),
        )


def gathered(shard, extents, number):
    rows, columns = shard.shape
    total = 2 * extents["z"] * extents["y"] * extents["x"]
    parts = row_parts(rows)
    order = route_order(parts, extents)
    slots = len(order)
    whole = pl.pallas_call(
        functools.partial(gather_kernel, extents, parts, order),
        out_shape=jax.ShapeDtypeStruct((total, rows, columns), shard.dtype),
        in_specs=[pl.BlockSpec(memory_space=pltpu.VMEM)],
        out_specs=pl.BlockSpec(memory_space=pl.ANY),
        scratch_shapes=[
            pltpu.SemaphoreType.DMA((slots,)),
            pltpu.SemaphoreType.DMA,
            pltpu.SemaphoreType.DMA,
            pltpu.SemaphoreType.DMA((len(parts), 2)),
            pltpu.SemaphoreType.DMA((slots, 2)),
            pltpu.SemaphoreType.DMA,
        ],
        compiler_params=pltpu.CompilerParams(collective_id=number, has_side_effects=True),
    )(shard)
    return whole.reshape(total * rows, columns)


CHILD_SEM = {("z", 1): 0, ("z", -1): 1, ("x", 0): 2, ("y", 0): 3}


def route_parent(slot):
    def up(dims):
        last = max(i for i, dim in enumerate(dims) if slot[dim] != 0)
        dim = dims[last]
        if dim != "z":
            return (dim, 0, 0, dict(slot, **{dim: 0}))
        side = 1 if slot["z"] > 0 else -1
        return (dim, side, -side, dict(slot, z=slot["z"] - side))

    return up


def child_rooms(dims, extents):
    rooms, base = ({}, 0)
    for i, dim in enumerate(dims):
        names = dims[:i] + (("z",) if dim == "z" else ())
        size = 1
        for name in names:
            size = size * extents[name]
        for side in (1, -1) if dim == "z" else (0,):
            rooms[dim, side] = (base, names)
            base = base + size
    return (rooms, base)


def small_steps(place, small_ref, total_ref, room_ref, small_got, small_sent):
    axes = ["core", "x", "y", "z"]
    spot = {"core": place.core, "x": place.x, "y": place.y, "z": place.z}
    count = dict(place.extents, core=2)

    def peer(dim, other):
        if dim == "z":
            return (other * 2 + place.core, place.ctx)
        return place.neighbour(dim, 0)

    def send(level):
        dim = axes[level]
        mine = spot[dim]
        source = small_ref if level == 0 else total_ref.at[level - 1]
        room_ref[level, mine] = source[...]
        for other in range(count[dim]):
            copy = pltpu.make_async_remote_copy(
                src_ref=source,
                dst_ref=room_ref.at[level, mine],
                send_sem=small_sent.at[level, other],
                recv_sem=small_got.at[level, mine],
                device_id=peer(dim, other),
                device_id_type=MESH,
            )
            pl.when(mine != other)(copy.start)

    def finish(level):
        dim = axes[level]
        mine = spot[dim]
        for other in range(count[dim]):
            room = room_ref.at[level, other]
            pl.when(mine != other)(functools.partial(drain, room, small_got.at[level, other]))
        value = room_ref[level, 0]
        for other in range(1, count[dim]):
            value = value + room_ref[level, other]
        total_ref[level] = value
        if level + 1 < len(axes):
            send(level + 1)

    def close():
        for level, dim in enumerate(axes):
            for other in range(count[dim]):
                pl.when(spot[dim] != other)(
                    functools.partial(drain, room_ref.at[level, 0], small_sent.at[level, other])
                )

    return (send, finish, close)


def scatter_kernel(extents, parts, order, small, border, *refs):
    left_ref, right_ref, refs = (refs[0], refs[1], refs[2:])
    if small:
        small_ref, out_ref, total_ref, refs = (refs[0], refs[1], refs[2], refs[3:])
    else:
        out_ref, refs = (refs[0], refs[1:])
    count = len(parts)
    stages, sides, owns, rooms, accs = [refs[i * count : (i + 1) * count] for i in range(5)]
    side_got, child_got, side_sent, sent = refs[5 * count : 5 * count + 4]
    place = Place(extents)
    chips = extents["z"] * extents["y"] * extents["x"]
    high, columns = (left_ref.shape[1], right_ref.shape[1])
    rank = {}
    for part, (_, _, dims) in enumerate(parts):
        for slot in route_slots(dims, extents):
            rank[part, slot_key(slot)] = len(rank)
    place.greet(whole=small)
    if small:
        send, finish, close = small_steps(place, small_ref, total_ref, *refs[5 * count + 4 :])
        send(0)

    def product(shard):
        left = left_ref[shard].astype(jnp.float32)
        line = lax.broadcasted_iota(jnp.int32, (high, 1), 0) + shard * high
        early = jnp.where(line < border, 1.0, 0.0)
        wide = jnp.concatenate([left * early, left * (1.0 - early)], axis=1)
        return dot(wide.astype(jnp.bfloat16), right_ref[...]).astype(jnp.bfloat16)

    def spread(turn, carry):
        z = (place.z + extents["z"] // 2 + turn // 4) % extents["z"]
        y = (place.y + 1 + (turn // 2) % 2) % 2
        x = (place.x + 1 + turn % 2) % 2
        chip = (z * 2 + y) * 2 + x
        theirs = product(((z * 2 + 1 - place.core) * 2 + y) * 2 + x)
        for part, (start, rows, _) in enumerate(parts):
            stages[part][chip] = theirs[start : start + rows]
            pltpu.make_async_remote_copy(
                src_ref=stages[part].at[chip],
                dst_ref=sides[part].at[chip],
                send_sem=side_sent.at[part],
                recv_sem=side_got.at[part, chip],
                device_id=place.neighbour("core", 0),
                device_id_type=MESH,
            ).start()
        mine = product(((z * 2 + place.core) * 2 + y) * 2 + x)
        for part, (start, rows, _) in enumerate(parts):
            owns[part][chip] = mine[start : start + rows]
        return carry

    def room_index(part, slot, dim, side):
        z, y, x = place.source(slot)
        spot = {"z": z, "y": y, "x": x}
        base, names = child_rooms(parts[part][2], extents)[0][dim, side]
        index = 0
        for name in names:
            index = index * extents[name] + spot[name]
        return base + index

    def by_columns(body):
        def one(turn, carry):
            body(pl.ds(pl.multiple_of(turn * 128, 128), 128))
            return carry

        lax.fori_loop(0, columns // 128, one, 0)

    def merge(part, key):
        start, rows, dims = parts[part]
        slot = dict(zip(("z", "y", "x"), key))
        number = rank[part, key]

        def step():
            chip = place.chip_index(slot)
            side, own, acc = (sides[part].at[chip], owns[part].at[chip], accs[part])
            found = [
                (
                    rooms[part].at[room_index(part, slot, dim, sign)],
                    child_got.at[number, CHILD_SEM[dim, sign]],
                    place.has(dim, sign),
                )
                for dim, sign, _ in route_children(slot, dims, extents)
            ]
            sure = [room for room, _, near in found if near is None]
            maybe = [one for one in found if one[2] is not None]
            drain(side, side_got.at[part, chip])
            for room, got, near in found:
                if near is None:
                    drain(room, got)
            last = key == (0, 0, 0)

            def settle(value, cut):
                if maybe:
                    acc[:, cut] = value
                elif last:
                    out_ref[pl.ds(start, rows), cut] = value
                else:
                    side[:, cut] = value.astype(jnp.bfloat16)

            def base(cut):
                value = own[:, cut].astype(jnp.float32) + side[:, cut].astype(jnp.float32)
                for room in sure:
                    value = value + room[:, cut].astype(jnp.float32)
                settle(value, cut)

            by_columns(base)
            for room, got, near in maybe:

                def take(room=room, got=got):
                    drain(room, got)

                    def more(cut):
                        acc[:, cut] += room[:, cut].astype(jnp.float32)

                    by_columns(more)

                pl.when(near)(take)
            if maybe:

                def close_up(cut):
                    if last:
                        out_ref[pl.ds(start, rows), cut] = acc[:, cut]
                    else:
                        side[:, cut] = acc[:, cut].astype(jnp.bfloat16)

                by_columns(close_up)
            if last:
                return
            dim, sign, seen, parent = route_parent(slot)(dims)
            pltpu.make_async_remote_copy(
                src_ref=side,
                dst_ref=rooms[part].at[room_index(part, slot, dim, seen)],
                send_sem=sent.at[part],
                recv_sem=child_got.at[rank[part, slot_key(parent)], CHILD_SEM[dim, seen]],
                device_id=place.neighbour(dim, sign),
                device_id_type=MESH,
            ).start()

        guarded(place.valid(slot), step)

    lax.fori_loop(0, chips, spread, 0)
    for i, one in enumerate(order):
        merge(*one)
        if small and (i + 1) % (len(order) // 5) == 0 and (i + 1) // (len(order) // 5) <= 4:
            finish((i + 1) // (len(order) // 5) - 1)
    if small:
        close()
    for part in range(count):
        drain(stages[part], side_sent.at[part])
        drain(sides[part].at[pl.ds(0, chips - 1)], sent.at[part])


def scattered(left, right, border, small, extents, number):
    total, rows, depth = left.shape
    columns = right.shape[1]
    chips = total // 2
    parts = row_parts(rows)
    order = list(reversed(route_order(parts, extents)))
    slots = len(order)
    vmem = pl.BlockSpec(memory_space=pltpu.VMEM)
    args = (left, right)
    outs = [jax.ShapeDtypeStruct((rows, columns), jnp.float32)]
    scratch = (
        [pltpu.VMEM((chips, size, columns), jnp.bfloat16) for _, size, _ in parts] * 3
        + [
            pltpu.VMEM((child_rooms(dims, extents)[1], size, columns), jnp.bfloat16)
            for _, size, dims in parts
        ]
        + [pltpu.VMEM((size, columns), jnp.float32) for _, size, _ in parts]
        + [
            pltpu.SemaphoreType.DMA((len(parts), chips)),
            pltpu.SemaphoreType.DMA((slots, 4)),
            pltpu.SemaphoreType.DMA((len(parts),)),
            pltpu.SemaphoreType.DMA((len(parts),)),
        ]
    )
    if small is not None:
        args = args + (small,)
        outs.append(jax.ShapeDtypeStruct((4,) + small.shape, jnp.float32))
        most = max(2, extents["z"])
        scratch = scratch + [
            pltpu.VMEM((4, most) + small.shape, jnp.float32),
            pltpu.SemaphoreType.DMA((4, most)),
            pltpu.SemaphoreType.DMA((4, most)),
        ]
    return pl.pallas_call(
        functools.partial(scatter_kernel, extents, parts, order, small is not None, border),
        out_shape=outs,
        in_specs=[vmem] * len(args),
        out_specs=[vmem] * len(outs),
        scratch_shapes=scratch,
        compiler_params=pltpu.CompilerParams(
            collective_id=number, has_side_effects=True, vmem_limit_bytes=56 * 1024 * 1024
        ),
    )(*args)


def routed():
    return lax.axis_size("ctx") == 4 and lax.axis_size("dp") % 2 == 0


def route_extents():
    return {"z": lax.axis_size("dp") // 2, "y": 2, "x": 2}


def all_rows(shard, number):
    if routed():
        return gathered(shard, route_extents(), number)
    return lax.all_gather(shard, ("dp", "ctx"), axis=0, tiled=True)


def owner_sums(first_left, first_right, second_left, second_right, small, number):
    if not routed():
        grad = to_owners(owner_rows(first_left, first_right, second_left, second_right))
        return (grad, None if small is None else lax.psum(small, ("dp", "ctx")))
    left = jnp.concatenate([first_left.T, second_left.T])
    border = first_left.shape[1]
    devices = lax.axis_size("dp") * lax.axis_size("ctx")
    left = left.reshape(devices, left.shape[0] // devices, left.shape[1])
    right = jnp.concatenate([first_right, second_right])
    if small is None:
        return (scattered(left, right, border, None, route_extents(), number)[0], None)
    extent = small.shape[0]
    rows = -(-extent // 1024) * 8
    packed = jnp.pad(small, (0, rows * 128 - extent)).reshape(rows, 128)
    grad, totals = scattered(left, right, border, packed, route_extents(), number)
    return (grad, totals[3].reshape(-1)[:extent])


def shifted(shard, by):
    return passed_along(shard, "ctx", by)


def per_device(
    inputs,
    segments,
    cotangent,
    mixer_params,
    mixer_first,
    mixer_second,
    feed_params,
    feed_first,
    feed_second,
    small_params,
    small_first,
    small_second,
):
    mixer_weights = all_rows(mixer_params.astype(jnp.bfloat16), 0)
    feed_half, mixer_weights = lax.optimization_barrier(
        (feed_params.astype(jnp.bfloat16), mixer_weights)
    )
    feed_weights = all_rows(feed_half, 1)
    conv_weight, gain_first, gain_second, out_gain, gate_rows, decay_log, decay_bias = unpack_small(
        small_params
    )
    channels = 2 * H * DK + H * DV
    input_rows = channels + H * DV
    margin = CONV - 1
    in_weight = mixer_weights[:input_rows]
    out_weight = mixer_weights[input_rows:]
    up_weight = feed_weights[: 2 * FF]
    down_weight = feed_weights[2 * FF :]
    tokens_here = inputs[0]
    cotangent_here = cotangent[0]
    token_count = tokens_here.shape[0]
    position = lax.axis_index("ctx") * token_count
    segment_padded = jnp.concatenate([jnp.full((margin,), -1, jnp.int32), segments[0]])
    segment_wide = lax.dynamic_slice_in_dim(segment_padded, position, token_count + margin)
    segment_ids = segment_wide[margin:]
    segment_before = segment_wide[margin - 1]
    inverse_first = lax.rsqrt(
        jnp.mean(tokens_here * tokens_here, axis=-1, keepdims=True) + EPS_NORM
    )
    normed = (tokens_here * inverse_first * gain_first).astype(jnp.bfloat16)
    gate_half = gate_rows.astype(jnp.bfloat16)
    logits = jnp.einsum("td,rd->tr", normed, gate_half, preferred_element_type=jnp.float32)
    rim_normed = shifted(normed[token_count - margin :], 1)
    projected = jnp.einsum(
        "td,rd->tr",
        jnp.concatenate([normed, rim_normed]),
        in_weight,
        preferred_element_type=jnp.float32,
    )
    rim_rows = projected[token_count:, :channels].astype(jnp.bfloat16)
    projected = projected[:token_count]
    conv_input = projected[:, :channels].astype(jnp.bfloat16)
    gate_pre = projected[:, channels:]
    extended = jnp.concatenate([rim_rows, conv_input]).astype(jnp.float32)

    active, active_back = jax.vjp(
        lambda wide, taps: active_rows(wide, taps, segment_wide), extended, conv_weight
    )
    span = min(SPAN, token_count)
    count = token_count // span
    scalars, scalars_back = jax.vjp(
        lambda *args: block_scalars(*args, segment_ids, segment_before, span),
        logits[:, :H],
        logits[:, H:],
        decay_log,
        decay_bias,
    )
    beta, running, carried, last = scalars
    segment_rows = jnp.broadcast_to(
        segment_ids.astype(jnp.float32).reshape(1, count, span), beta.shape
    )
    blank = jnp.zeros_like(beta)
    row_pack = jnp.stack(
        [beta, running, segment_rows, carried, last, blank, blank, blank], axis=2
    )
    column_pack = jnp.swapaxes(row_pack, 2, 3)
    groups = H // GROUP
    key_blocks = H * DK // (GROUP * DK)
    value_start = 2 * H * DK // (GROUP * DV)
    query_spec = pl.BlockSpec((span, GROUP * DK), lambda c, g: (c, g))
    key_spec = pl.BlockSpec((span, GROUP * DK), lambda c, g: (c, g + key_blocks))
    value_spec = pl.BlockSpec((span, GROUP * DV), lambda c, g: (c, g + value_start))
    wide_spec = pl.BlockSpec((span, GROUP * DV), lambda c, g: (c, g))
    row_spec = pl.BlockSpec((GROUP, 1, 8, span), lambda c, g: (g, c, 0, 0))
    column_spec = pl.BlockSpec((GROUP, 1, span, 8), lambda c, g: (g, c, 0, 0))
    inverse_spec = pl.BlockSpec((1, GROUP, span, span), lambda c, g: (c, g, 0, 0))
    square_spec = pl.BlockSpec((1, GROUP, DK, DK), lambda c, g: (c, g, 0, 0))
    state_spec = pl.BlockSpec((1, GROUP, DK, DV), lambda c, g: (c, g, 0, 0))
    gain_spec = pl.BlockSpec((1, DV), lambda c, g: (0, 0))
    key_out = ((token_count, H * DK), jnp.float32)
    value_out = ((token_count, H * DV), jnp.float32)
    state_out = ((count, H, DK, DV), jnp.float32)
    grid = (count, groups)
    inverse, w_part, u_part, r_part, o_part, transfers, offsets = kernel_call(
        block_kernel,
        grid,
        (active, active, active, row_pack, column_pack),
        [query_spec, key_spec, value_spec, row_spec, column_spec],
        [
            ((count, H, span, span), jnp.float32),
            key_out,
            value_out,
            key_out,
            value_out,
            ((count, H, DK, DK), jnp.float32),
            state_out,
        ],
        [inverse_spec, query_spec, wide_spec, query_spec, wide_spec, square_spec, state_spec],
    )

    def advance(left, right):
        return jnp.einsum(
            "hij,hjw->hiw", left, right, precision=CORE, preferred_element_type=jnp.float32
        )

    def advance_back(left, right):
        return jnp.einsum(
            "hji,hjw->hiw", left, right, precision=CORE, preferred_element_type=jnp.float32
        )

    transfer, offset_state = (transfers[0], offsets[0])
    for block in range(1, count):
        transfer = advance(transfers[block], transfer)
        offset_state = advance(transfers[block], offset_state) + offsets[block]
    ring = lax.axis_size("ctx")
    transfer_half = transfer.astype(jnp.bfloat16)
    offset_half = offset_state.astype(jnp.bfloat16)
    befores = [
        (shifted(transfer_half, by), shifted(offset_half, by)) for by in range(1, ring)
    ]
    state_in = jnp.zeros((H, DK, DV), jnp.float32)
    for transfer_there, offset_there in reversed(befores):
        state_in = advance(transfer_there.astype(jnp.float32), state_in) + offset_there
    states = [state_in]
    for block in range(count - 1):
        states.append(advance(transfers[block], states[-1]) + offsets[block])
    states = jnp.stack(states)
    gain_row = out_gain.reshape(1, DV)
    recurrent_out, mix_half = kernel_call(
        output_kernel,
        grid,
        (r_part, o_part, states, gate_pre, gain_row),
        [query_spec, wide_spec, state_spec, wide_spec, gain_spec],
        [value_out, ((token_count, H * DV), jnp.bfloat16)],
        [wide_spec, wide_spec],
    )
    afters = [shifted(transfer_half, -by) for by in range(1, ring)]
    hidden = tokens_here + jnp.dot(mix_half, out_weight, preferred_element_type=jnp.float32)
    inverse_second = lax.rsqrt(jnp.mean(hidden * hidden, axis=-1, keepdims=True) + EPS_NORM)
    hidden_normed = (hidden * inverse_second * gain_second).astype(jnp.bfloat16)
    gate_up = jnp.einsum("td,rd->tr", hidden_normed, up_weight, preferred_element_type=jnp.float32)
    gate_part = gate_up[:, :FF]
    up_part = gate_up[:, FF:]
    middle = (jax.nn.silu(gate_part) * up_part).astype(jnp.bfloat16)
    result = hidden + jnp.dot(middle, down_weight, preferred_element_type=jnp.float32)
    cotangent_half = cotangent_here.astype(jnp.bfloat16)
    grad_middle = jnp.einsum(
        "td,fd->tf", cotangent_half, down_weight, preferred_element_type=jnp.float32
    )
    sigmoid_gate = jax.nn.sigmoid(gate_part)
    grad_gate = (
        grad_middle * up_part * (sigmoid_gate + gate_part * sigmoid_gate * (1.0 - sigmoid_gate))
    )
    grad_up = grad_middle * gate_part * sigmoid_gate
    grad_gate_up = jnp.concatenate([grad_gate, grad_up], axis=1).astype(jnp.bfloat16)
    grad_hidden_normed = jnp.dot(grad_gate_up, up_weight, preferred_element_type=jnp.float32)
    grad_hidden = cotangent_here + norm_back(
        hidden, inverse_second, gain_second, grad_hidden_normed
    )
    grad_gain_second = jnp.sum(grad_hidden_normed * hidden * inverse_second, axis=0)
    grad_hidden_half = grad_hidden.astype(jnp.bfloat16)
    feed_grad, _ = owner_sums(grad_gate_up, hidden_normed, middle, cotangent_half, None, 2)
    grad_mix = jnp.einsum(
        "td,rd->tr", grad_hidden_half, out_weight, preferred_element_type=jnp.float32
    )
    partial_spec = pl.BlockSpec((1, 1, DV), lambda c, g: (c * groups + g, 0, 0))
    grad_recurrent, grad_gate_pre, gain_parts, locals_back = kernel_call(
        gate_back_kernel,
        grid,
        (grad_mix, recurrent_out, gate_pre, gain_row, r_part),
        [wide_spec, wide_spec, wide_spec, gain_spec, query_spec],
        [value_out, value_out, ((count * groups, 1, DV), jnp.float32), state_out],
        [wide_spec, wide_spec, partial_spec, state_spec],
    )
    grad_out_gain = jnp.sum(gain_parts, axis=(0, 1))
    local_part = locals_back[count - 1]
    for block in range(count - 2, -1, -1):
        local_part = advance_back(transfers[block], local_part) + locals_back[block]
    local_half = local_part.astype(jnp.bfloat16)
    local_afters = [shifted(local_half, -by) for by in range(1, ring)]
    state_grad = jnp.zeros((H, DK, DV), jnp.float32)
    for transfer_there, local_there in reversed(list(zip(afters, local_afters))):
        state_grad = advance_back(transfer_there.astype(jnp.float32), state_grad) + local_there
    nexts = [state_grad]
    for block in range(count - 1, 0, -1):
        nexts.append(advance_back(transfers[block], nexts[-1]) + locals_back[block])
    nexts = jnp.stack(nexts[::-1])
    grad_q, grad_k, grad_v, grad_row_pack, grad_column_pack = kernel_call(
        block_back_kernel,
        grid,
        (
            active,
            active,
            active,
            row_pack,
            column_pack,
            inverse,
            w_part,
            u_part,
            states,
            grad_recurrent,
            nexts,
        ),
        [
            query_spec,
            key_spec,
            value_spec,
            row_spec,
            column_spec,
            inverse_spec,
            query_spec,
            wide_spec,
            state_spec,
            wide_spec,
            state_spec,
        ],
        [key_out, key_out, value_out, (row_pack.shape, jnp.float32), (column_pack.shape, jnp.float32)],
        [query_spec, query_spec, wide_spec, row_spec, column_spec],
    )
    grad_pack = grad_row_pack + jnp.swapaxes(grad_column_pack, 2, 3)
    grad_beta_logit, grad_alpha_logit, grad_decay_log, grad_decay_bias = scalars_back(
        (grad_pack[:, :, 0], grad_pack[:, :, 1], grad_pack[:, :, 3], grad_pack[:, :, 4])
    )
    grad_wide, grad_conv = active_back(jnp.concatenate([grad_q, grad_k, grad_v], axis=1))
    back_rim = passed_along(grad_wide[:margin].astype(jnp.bfloat16), "ctx", -1).astype(jnp.float32)
    grad_conv_input = grad_wide[margin:]
    grad_conv_input = jnp.concatenate(
        [
            grad_conv_input[: token_count - margin],
            grad_conv_input[token_count - margin :] + back_rim,
        ]
    )
    grad_projected = jnp.concatenate([grad_conv_input, grad_gate_pre], axis=1).astype(jnp.bfloat16)
    grad_logits = jnp.concatenate([grad_beta_logit, grad_alpha_logit], axis=1).astype(jnp.bfloat16)
    grad_normed = jnp.dot(grad_projected, in_weight, preferred_element_type=jnp.float32)
    grad_normed = grad_normed + jnp.dot(grad_logits, gate_half, preferred_element_type=jnp.float32)
    grad_inputs = grad_hidden + norm_back(tokens_here, inverse_first, gain_first, grad_normed)
    grad_gain_first = jnp.sum(grad_normed * tokens_here * inverse_first, axis=0)
    gate_grad = jnp.einsum("tr,td->rd", grad_logits, normed, preferred_element_type=jnp.float32)
    small_local = jnp.concatenate(
        [
            grad_conv.reshape(-1),
            grad_gain_first,
            grad_gain_second,
            grad_out_gain,
            gate_grad.reshape(-1),
            grad_decay_log,
            grad_decay_bias,
        ]
    )
    mixer_grad, small_grad = owner_sums(
        grad_projected, normed, mix_half, grad_hidden_half, small_local, 3
    )
    mixer_new, mixer_moment, mixer_square = adamw(
        mixer_params, mixer_grad, mixer_first, mixer_second
    )
    feed_new, feed_moment, feed_square = adamw(feed_params, feed_grad, feed_first, feed_second)
    small_new, small_moment, small_square = adamw(
        small_params, small_grad, small_first, small_second
    )
    return (
        result[None],
        grad_inputs[None],
        mixer_grad,
        feed_grad,
        small_grad,
        mixer_new,
        mixer_moment,
        mixer_square,
        feed_new,
        feed_moment,
        feed_square,
        small_new,
        small_moment,
        small_square,
    )


def solution(mesh):
    in_specs = (
        P("dp", "ctx", None),
        P("dp", None),
        P("dp", "ctx", None),
        P(("dp", "ctx"), None),
        P(("dp", "ctx"), None),
        P(("dp", "ctx"), None),
        P(("dp", "ctx"), None),
        P(("dp", "ctx"), None),
        P(("dp", "ctx"), None),
        P(),
        P(),
        P(),
    )
    out_specs = (
        P("dp", "ctx", None),
        P("dp", "ctx", None),
        P(("dp", "ctx"), None),
        P(("dp", "ctx"), None),
        P(),
        P(("dp", "ctx"), None),
        P(("dp", "ctx"), None),
        P(("dp", "ctx"), None),
        P(("dp", "ctx"), None),
        P(("dp", "ctx"), None),
        P(("dp", "ctx"), None),
        P(),
        P(),
        P(),
    )
    return jax.shard_map(
        per_device, mesh=mesh, in_specs=in_specs, out_specs=out_specs, check_vma=False
    )
```

```python
import functools
import heapq

import jax
import jax.numpy as jnp
from jax import lax
from jax.experimental import pallas as pl
from jax.experimental.pallas import tpu as pltpu
from jax.sharding import PartitionSpec as P

D = 1024
H = 8
DK = 128
DV = 256
FF = 2816
CONV = 4
SPAN = 128
GROUP = 4
STEP = 10


PRECISE = lax.Precision.HIGHEST
CORE = lax.Precision.DEFAULT
EPS_NORM = 1e-06
EPS_GATE = 1e-05
EPS_KEYS = 1e-06
LEARN_RATE = 0.002
FIRST_RATE = 0.9
SECOND_RATE = 0.95
EPS_ADAM = 1e-08
WEIGHT_DECAY = 0.1


def passed_along(shard, axis, by):
    count = lax.axis_size(axis)
    pairs = [(i, i + by) for i in range(count) if 0 <= i + by < count]
    return lax.ppermute(shard, axis, pairs)


def dot(left, right, contract=((1,), (0,)), precision=None):
    return lax.dot_general(
        left, right, (contract, ((), ())), precision=precision, preferred_element_type=jnp.float32
    )


def unit_rows(raw, scale):
    inverse = lax.rsqrt(jnp.sum(raw * raw, axis=-1, keepdims=True) + EPS_KEYS)
    return (raw * (inverse * scale), inverse)


def unit_back(raw, inverse, scale, upstream):
    upstream = upstream * scale
    shared = jnp.sum(raw * upstream, axis=-1, keepdims=True)
    return inverse * upstream - raw * (inverse * inverse * inverse * shared)


def block_decays(rows, columns, extent):
    places = lax.broadcasted_iota(jnp.int32, (extent, extent), 0)
    others = lax.broadcasted_iota(jnp.int32, (extent, extent), 1)
    keep = (columns[:, 2:3] == rows[2:3, :]) & (places >= others)
    spread = jnp.minimum(columns[:, 1:2] - rows[1:2, :], 0.0)
    return (jnp.where(keep, jnp.exp(spread), 0.0), places, others)


def block_kernel(
    q_ref, k_ref, v_ref, row_ref, column_ref,
    inverse_ref, w_ref, u_ref, r_ref, o_ref, transfer_ref, offset_ref,
):
    group = row_ref.shape[0]
    extent = q_ref.shape[0]
    systems, solved, pieces = ([], [], [])
    for h in range(group):
        rows, columns = (row_ref[h, 0], column_ref[h, 0])
        keys = slice(h * DK, (h + 1) * DK)
        queries, _ = unit_rows(q_ref[:, keys], DK ** (-0.5))
        key_rows, _ = unit_rows(k_ref[:, keys], 1.0)
        decays, places, others = block_decays(rows, columns, extent)
        weighted = decays * rows[0:1, :]
        key_key = dot(key_rows, key_rows, ((1,), (1,)), CORE)
        system = jnp.where(places > others, weighted * key_key, 0.0)
        apart = places ^ others
        systems.append(system)
        solved.append(
            jnp.where(places == others, 1.0, 0.0) - jnp.where(apart < 2, system, 0.0)
        )
        mixing = weighted * dot(queries, key_rows, ((1,), (1,)), CORE)
        pieces.append((queries, key_rows, mixing, columns))
    size = 2
    while size < extent:
        level = (apart >= size) & (apart < 2 * size)
        halves = [
            dot(solved[h], jnp.where(level, systems[h], 0.0), precision=PRECISE)
            for h in range(group)
        ]
        solved = [
            solved[h] - dot(halves[h], solved[h], precision=PRECISE) for h in range(group)
        ]
        size = 2 * size
    for h in range(group):
        queries, key_rows, mixing, columns = pieces[h]
        keys = slice(h * DK, (h + 1) * DK)
        values = slice(h * DV, (h + 1) * DV)
        carried = columns[:, 3:4]
        inverse_ref[0, h] = solved[h]
        w_part = dot(solved[h], carried * key_rows, precision=CORE)
        u_part = dot(solved[h], v_ref[:, values], precision=CORE)
        w_ref[:, keys] = w_part
        u_ref[:, values] = u_part
        r_ref[:, keys] = carried * queries - dot(mixing, w_part, precision=CORE)
        o_ref[:, values] = dot(mixing, u_part, precision=CORE)
        last_keys = key_rows * columns[:, 4:5]
        rank = lax.broadcasted_iota(jnp.int32, (DK, DK), 0)
        file = lax.broadcasted_iota(jnp.int32, (DK, DK), 1)
        transfer_ref[0, h] = jnp.where(
            rank == file, carried[extent - 1 : extent, :], 0.0
        ) - dot(last_keys, w_part, ((0,), (0,)), CORE)
        offset_ref[0, h] = dot(last_keys, u_part, ((0,), (0,)), CORE)


def output_kernel(r_ref, o_ref, state_ref, gate_ref, gain_ref, recurrent_ref, mix_ref):
    for h in range(state_ref.shape[1]):
        keys = slice(h * DK, (h + 1) * DK)
        values = slice(h * DV, (h + 1) * DV)
        recurrent = o_ref[:, values] + dot(r_ref[:, keys], state_ref[0, h], precision=CORE)
        recurrent_ref[:, values] = recurrent
        inverse = lax.rsqrt(jnp.mean(recurrent * recurrent, axis=-1, keepdims=True) + EPS_GATE)
        mix_ref[:, values] = (
            recurrent * inverse * gain_ref[...] * jax.nn.silu(gate_ref[:, values])
        ).astype(jnp.bfloat16)


def gate_back_kernel(
    mix_ref, recurrent_ref, gate_ref, gain_ref, r_ref,
    grad_ref, grad_gate_ref, grad_gain_ref, local_ref,
):
    total = jnp.zeros((1, DV), jnp.float32)
    for h in range(local_ref.shape[1]):
        keys = slice(h * DK, (h + 1) * DK)
        values = slice(h * DV, (h + 1) * DV)
        upstream, recurrent, gate = (mix_ref[:, values], recurrent_ref[:, values], gate_ref[:, values])
        inverse = lax.rsqrt(jnp.mean(recurrent * recurrent, axis=-1, keepdims=True) + EPS_GATE)
        normal = recurrent * inverse
        sig = jax.nn.sigmoid(gate)
        gain = gain_ref[...]
        grad_gate_ref[:, values] = upstream * normal * gain * (sig + gate * sig * (1.0 - sig))
        scaled = upstream * (gate * sig)
        total = total + jnp.sum(scaled * normal, axis=0, keepdims=True)
        scaled = scaled * gain
        grad = inverse * (scaled - normal * jnp.mean(scaled * normal, axis=-1, keepdims=True))
        grad_ref[:, values] = grad
        local_ref[0, h] = dot(r_ref[:, keys], grad, ((0,), (0,)), CORE)
    grad_gain_ref[0] = total


def block_back_kernel(
    q_ref, k_ref, v_ref, row_ref, column_ref, inverse_ref, w_ref, u_ref, state_ref, grad_ref, next_ref,
    grad_q_ref, grad_k_ref, grad_v_ref, grad_row_ref, grad_column_ref,
):
    group = row_ref.shape[0]
    extent = q_ref.shape[0]
    for h in range(group):
        rows, columns = (row_ref[h, 0], column_ref[h, 0])
        keys = slice(h * DK, (h + 1) * DK)
        values = slice(h * DV, (h + 1) * DV)
        raw_q, raw_k = (q_ref[:, keys], k_ref[:, keys])
        queries, inverse_q = unit_rows(raw_q, DK ** (-0.5))
        key_rows, inverse_k = unit_rows(raw_k, 1.0)
        decays, places, others = block_decays(rows, columns, extent)
        beta = rows[0:1, :]
        carried, last = (columns[:, 3:4], columns[:, 4:5])
        weighted = decays * beta
        strict = places > others
        key_key = dot(key_rows, key_rows, ((1,), (1,)), CORE)
        query_key = dot(queries, key_rows, ((1,), (1,)), CORE)
        state, upstream, after = (state_ref[0, h], grad_ref[:, values], next_ref[0, h])
        delta = u_ref[:, values] - dot(w_ref[:, keys], state, precision=CORE)
        grad_delta = dot(weighted * query_key, upstream, ((0,), (0,)), CORE) + dot(
            key_rows * last, after, precision=CORE
        )
        grad_mixing = dot(upstream, delta, ((1,), (1,)), CORE)
        grad_target = dot(inverse_ref[0, h], grad_delta, ((0,), (0,)), CORE)
        grad_system = jnp.where(strict, -dot(grad_target, delta, ((1,), (1,)), CORE), 0.0)
        up_state = dot(upstream, state, ((1,), (1,)), CORE)
        down_state = dot(grad_target, state, ((1,), (1,)), CORE)
        grad_last = dot(delta, after, ((1,), (1,)), CORE)
        grad_carried = jnp.sum(up_state * queries - down_state * key_rows, axis=-1, keepdims=True)
        line = lax.broadcasted_iota(jnp.int32, (extent, 1), 0)
        grad_carried = grad_carried + jnp.where(
            line == extent - 1, jnp.sum(after * state, keepdims=True), 0.0
        )
        grad_qk = grad_mixing * weighted
        grad_kk = grad_system * weighted
        grad_queries = carried * up_state + dot(grad_qk, key_rows, precision=CORE)
        grad_keys = (
            grad_last * last
            - carried * down_state
            + dot(grad_qk, queries, ((0,), (0,)), CORE)
            + dot(grad_kk, key_rows, precision=CORE)
            + dot(grad_kk, key_rows, ((0,), (0,)), CORE)
        )
        grad_q_ref[:, keys] = unit_back(raw_q, inverse_q, DK ** (-0.5), grad_queries)
        grad_k_ref[:, keys] = unit_back(raw_k, inverse_k, 1.0, grad_keys)
        grad_v_ref[:, values] = grad_target
        spread = (grad_system * key_key + grad_mixing * query_key) * decays
        grad_row_ref[h, 0] = jnp.zeros_like(rows)
        grad_row_ref[h, 0, 0:1, :] = jnp.sum(spread, axis=0, keepdims=True)
        grad_row_ref[h, 0, 1:2, :] = -jnp.sum(spread * beta, axis=0, keepdims=True)
        place = lax.broadcasted_iota(jnp.int32, (extent, 8), 1)
        grad_column_ref[h, 0] = jnp.where(
            place == 1,
            jnp.sum(spread * beta, axis=-1, keepdims=True),
            jnp.where(
                place == 3,
                grad_carried,
                jnp.where(
                    place == 4, jnp.sum(grad_last * key_rows, axis=-1, keepdims=True), 0.0
                ),
            ),
        )


def block_scalars(beta_logit, alpha_logit, decay_log, decay_bias, segment_ids, segment_before, span):
    token_count = beta_logit.shape[0]
    count = token_count // span
    beta = jax.nn.sigmoid(beta_logit)
    log_decay = -jnp.exp(decay_log) * jax.nn.softplus(alpha_logit + decay_bias)

    def blocks(tensor):
        return tensor.T.reshape(H, count, span)

    beta, log_decay = (blocks(beta), blocks(log_decay))
    segment_blocks = segment_ids.reshape(count, span)
    befores = jnp.concatenate([jnp.reshape(segment_before, (1,)), segment_blocks[:-1, -1]])
    upper = (jnp.arange(span)[:, None] <= jnp.arange(span)[None, :]).astype(jnp.float32)
    running = jnp.einsum("hcs,st->hct", log_decay, upper, precision=PRECISE)
    carried = jnp.where((segment_blocks == befores[:, None])[None], jnp.exp(running), 0.0)
    ending = (segment_blocks == segment_blocks[:, -1:])[None]
    last = jnp.where(ending, jnp.exp(jnp.minimum(running[:, :, -1:] - running, 0.0)), 0.0) * beta
    return (beta, running, carried, last)


def kernel_call(body, grid, args, in_specs, outs, out_specs):
    return pl.pallas_call(
        body,
        grid=grid,
        in_specs=in_specs,
        out_specs=out_specs,
        out_shape=[jax.ShapeDtypeStruct(shape, dtype) for shape, dtype in outs],
        compiler_params=pltpu.CompilerParams(vmem_limit_bytes=48 * 1024 * 1024),
    )(*args)


def active_rows(extended, conv_weight, segment_wide):
    margin = CONV - 1
    token_count = extended.shape[0] - margin
    segment_ids = segment_wide[margin:]
    mixed = jnp.zeros((token_count, extended.shape[1]), extended.dtype)
    for offset in range(CONV):
        start_row = margin - offset
        window = extended[start_row : start_row + token_count]
        keep_mask = (segment_wide[start_row : start_row + token_count] == segment_ids)[:, None]
        mixed = mixed + jnp.where(keep_mask, window * conv_weight[offset], 0.0)
    return jax.nn.silu(mixed)


def norm_back(values, inverse, gain_row, upstream):
    weighted = gain_row * upstream
    return inverse * weighted - values * inverse**3 * jnp.mean(
        weighted * values, axis=-1, keepdims=True
    )


def unpack_small(packed):
    channels = 2 * H * DK + H * DV
    bounds = [CONV * channels, D, D, DV, 2 * H * D, H, H]
    pieces = []
    cursor = 0
    for extent in bounds:
        pieces.append(packed[cursor : cursor + extent])
        cursor = cursor + extent
    return (
        pieces[0].reshape(CONV, channels),
        pieces[1],
        pieces[2],
        pieces[3],
        pieces[4].reshape(2 * H, D),
        pieces[5],
        pieces[6],
    )


def adamw(current, gradient, moment, square):
    moment = FIRST_RATE * moment + (1.0 - FIRST_RATE) * gradient
    square = SECOND_RATE * square + (1.0 - SECOND_RATE) * gradient * gradient
    update = (
        moment
        / (1.0 - FIRST_RATE**STEP)
        / (jnp.sqrt(square / (1.0 - SECOND_RATE**STEP)) + EPS_ADAM)
    )
    return (current - LEARN_RATE * (update + WEIGHT_DECAY * current), moment, square)


def owner_rows(first_left, first_right, second_left, second_right):
    def product(left_part, right_part):
        return jnp.einsum(
            "tr,td->rd", left_part, right_part, preferred_element_type=jnp.float32
        ).astype(jnp.bfloat16)

    return jnp.concatenate(
        [product(first_left, first_right), product(second_left, second_right)], axis=0
    )


def to_owners(rows):
    return lax.psum_scatter(rows, ("dp", "ctx"), scatter_dimension=0, tiled=True).astype(
        jnp.float32
    )


def ranks_of(extent):
    return [0] + [side * step for step in range(1, extent) for side in (1, -1)]


def route_slots(order, extents):
    found = [{}]
    for dim in order:
        values = ranks_of(extents[dim]) if dim == "z" else list(range(extents[dim]))
        found = [dict(one, **{dim: value}) for one in found for value in values]
    return found


def slot_key(slot):
    return (slot["z"], slot["y"], slot["x"])


def route_children(slot, order, extents):
    reached = max([i for i, dim in enumerate(order) if slot[dim] != 0], default=-1)
    found = []
    for i, dim in enumerate(order):
        if i < reached:
            continue
        if dim == "z":
            sides = (1, -1) if i > reached else ((-1,) if slot["z"] > 0 else (1,))
            for side in sides:
                child = dict(slot, z=slot["z"] - side)
                if abs(child["z"]) < extents["z"]:
                    found.append((dim, side, child))
        elif i > reached:
            found.append((dim, 0, dict(slot, **{dim: 1})))
    return found


def route_order(parts, extents):
    chips = [
        (z, y, x) for z in range(extents["z"]) for y in range(extents["y"]) for x in range(extents["x"])
    ]
    free, events, seen = ({}, [], {})
    for chip in chips:
        for part in range(len(parts)):
            events.append((0.0, chip, part, (0, 0, 0)))
    heapq.heapify(events)
    while events:
        now, chip, part, key = heapq.heappop(events)
        seen.setdefault((part, key), []).append(now)
        slot = dict(zip(("z", "y", "x"), key))
        for dim, side, child in route_children(slot, parts[part][2], extents):
            if dim == "z":
                there = (chip[0] + side, chip[1], chip[2])
                if not 0 <= there[0] < extents["z"]:
                    continue
            elif dim == "y":
                there = (chip[0], 1 - chip[1], chip[2])
            else:
                there = (chip[0], chip[1], 1 - chip[2])
            end = max(now, free.get((chip, there), 0.0)) + parts[part][1]
            free[chip, there] = end
            heapq.heappush(events, (end + 22.0, there, part, slot_key(child)))
    return sorted(seen, key=lambda one: (sum(seen[one]) / len(seen[one]), one))


def row_parts(rows):
    first = (rows * 3 // 8) // 16 * 16
    second = (rows * 7 // 16) // 16 * 16
    return [
        (0, first, ("z", "x", "y")),
        (first, second, ("z", "y", "x")),
        (first + second, rows - first - second, ("x", "y", "z")),
    ]


class Place:
    def __init__(self, extents):
        dp, ctx = (lax.axis_index("dp"), lax.axis_index("ctx"))
        self.extents = extents
        self.z, self.core = (dp // 2, dp % 2)
        self.y, self.x = (ctx // 2, ctx % 2)
        self.dp, self.ctx = (dp, ctx)

    def valid(self, slot):
        if slot["z"] == 0:
            return None
        z = self.z + slot["z"]
        return (z >= 0) & (z < self.extents["z"])

    def source(self, slot):
        y = self.y if slot["y"] == 0 else 1 - self.y
        x = self.x if slot["x"] == 0 else 1 - self.x
        return (self.z + slot["z"], y, x)

    def chip_index(self, slot):
        z, y, x = self.source(slot)
        return (z * 2 + y) * 2 + x

    def shard_index(self, slot, core):
        z, y, x = self.source(slot)
        return ((z * 2 + core) * 2 + y) * 2 + x

    def neighbour(self, dim, side):
        if dim == "z":
            return (self.dp + 2 * side, self.ctx)
        if dim == "core":
            return (self.dp + 1 - 2 * self.core, self.ctx)
        if dim == "y":
            return (self.dp, (1 - self.y) * 2 + self.x)
        return (self.dp, self.y * 2 + 1 - self.x)

    def has(self, dim, side):
        if dim != "z":
            return None
        return (self.z + side < self.extents["z"]) if side > 0 else (self.z + side >= 0)

    def greet(self, whole=False):
        barrier = pltpu.get_barrier_semaphore()
        total = 3
        for dim in ("core", "x", "y"):
            pl.semaphore_signal(barrier, 1, device_id=self.neighbour(dim, 0), device_id_type=MESH)
        if whole:
            for z in range(self.extents["z"]):

                @pl.when(self.z != z)
                def _():
                    pl.semaphore_signal(
                        barrier, 1, device_id=(2 * z + self.core, self.ctx), device_id_type=MESH
                    )

            total = total + self.extents["z"] - 1
        else:
            for side in (1, -1):
                near = self.has("z", side)

                @pl.when(near)
                def _():
                    pl.semaphore_signal(
                        barrier, 1, device_id=self.neighbour("z", side), device_id_type=MESH
                    )

                total = total + near.astype(jnp.int32)
        pl.semaphore_wait(barrier, total)


MESH = pl.DeviceIdType.MESH


def both(left, right):
    if left is None:
        return right
    return left if right is None else left & right


def guarded(condition, body):
    if condition is None:
        body()
    else:
        pl.when(condition)(body)


def drain(ref, sem):
    pltpu.make_async_copy(ref, ref, sem).wait()


def gather_kernel(
    extents, parts, order, shard_ref, out_ref, got, side_got, side_sent, flat_sent, z_sent, own_sem
):
    place = Place(extents)
    chips = extents["z"] * extents["y"] * extents["x"]
    rank = {}
    for part, (_, _, dims) in enumerate(parts):
        for slot in route_slots(dims, extents):
            rank[part, slot_key(slot)] = len(rank)
    place.greet()
    mine = place.shard_index({"z": 0, "y": 0, "x": 0}, place.core)
    own = pltpu.make_async_copy(shard_ref, out_ref.at[mine], own_sem)
    own.start()
    waits = []
    for part, key in order:
        start, rows, dims = parts[part]
        slot = dict(zip(("z", "y", "x"), key))
        number = rank[part, key]

        def step(part=part, key=key, start=start, rows=rows, dims=dims, slot=slot, number=number):
            block = out_ref.at[place.shard_index(slot, place.core), pl.ds(start, rows)]
            held = shard_ref.at[pl.ds(start, rows)] if key == (0, 0, 0) else block
            if key != (0, 0, 0):
                drain(block, got.at[number])
            for dim, side, child in route_children(slot, dims, extents):
                there = rank[part, slot_key(child)]
                if dim == "z":
                    sent = z_sent.at[number, (side + 1) // 2]
                else:
                    sent = flat_sent.at[part, 0 if dim == "x" else 1]
                copy = pltpu.make_async_remote_copy(
                    src_ref=held,
                    dst_ref=block,
                    send_sem=sent,
                    recv_sem=got.at[there],
                    device_id=place.neighbour(dim, side),
                    device_id_type=MESH,
                )
                guarded(place.has(dim, side), copy.start)
            pltpu.make_async_remote_copy(
                src_ref=held,
                dst_ref=block,
                send_sem=side_sent,
                recv_sem=side_got,
                device_id=place.neighbour("core", 0),
                device_id_type=MESH,
            ).start()

        guarded(place.valid(slot), step)
        for dim, side, _ in route_children(slot, dims, extents):
            if dim == "z":
                waits.append((slot, side, start, rows, z_sent.at[number, (side + 1) // 2]))
    own.wait()
    drain(out_ref.at[pl.ds(0, chips)], side_got)
    drain(out_ref.at[pl.ds(0, chips)], side_sent)
    for part, (start, rows, dims) in enumerate(parts):
        counts = {"x": 0, "y": 0}
        for slot in route_slots(dims, extents):
            if slot["z"] < 0:
                continue
            for dim, _, _ in route_children(slot, dims, extents):
                if dim != "z":
                    counts[dim] = counts[dim] + 1
        for dim in ("x", "y"):
            drain(
                out_ref.at[pl.ds(0, counts[dim]), pl.ds(start, rows)],
                flat_sent.at[part, 0 if dim == "x" else 1],
            )
    for slot, side, start, rows, sent in waits:
        guarded(
            both(place.valid(slot), place.has("z", side)),
            functools.partial(drain, out_ref.at[0, pl.ds(start, rows)], sent),
        )


def gathered(shard, extents, number):
    rows, columns = shard.shape
    total = 2 * extents["z"] * extents["y"] * extents["x"]
    parts = row_parts(rows)
    order = route_order(parts, extents)
    slots = len(order)
    whole = pl.pallas_call(
        functools.partial(gather_kernel, extents, parts, order),
        out_shape=jax.ShapeDtypeStruct((total, rows, columns), shard.dtype),
        in_specs=[pl.BlockSpec(memory_space=pltpu.VMEM)],
        out_specs=pl.BlockSpec(memory_space=pl.ANY),
        scratch_shapes=[
            pltpu.SemaphoreType.DMA((slots,)),
            pltpu.SemaphoreType.DMA,
            pltpu.SemaphoreType.DMA,
            pltpu.SemaphoreType.DMA((len(parts), 2)),
            pltpu.SemaphoreType.DMA((slots, 2)),
            pltpu.SemaphoreType.DMA,
        ],
        compiler_params=pltpu.CompilerParams(collective_id=number, has_side_effects=True),
    )(shard)
    return whole.reshape(total * rows, columns)


CHILD_SEM = {("z", 1): 0, ("z", -1): 1, ("x", 0): 2, ("y", 0): 3}


def route_parent(slot):
    def up(dims):
        last = max(i for i, dim in enumerate(dims) if slot[dim] != 0)
        dim = dims[last]
        if dim != "z":
            return (dim, 0, 0, dict(slot, **{dim: 0}))
        side = 1 if slot["z"] > 0 else -1
        return (dim, side, -side, dict(slot, z=slot["z"] - side))

    return up


def child_rooms(dims, extents):
    rooms, base = ({}, 0)
    for i, dim in enumerate(dims):
        names = dims[:i] + (("z",) if dim == "z" else ())
        size = 1
        for name in names:
            size = size * extents[name]
        for side in (1, -1) if dim == "z" else (0,):
            rooms[dim, side] = (base, names)
            base = base + size
    return (rooms, base)


def small_steps(place, small_ref, total_ref, *refs):
    work, half, quarter, eighth, line, got, sent = refs
    depth = place.extents["z"]
    fours = place.core * 4
    twos = fours + place.x * 2
    one = twos + place.y
    swaps = [
        ("core", fours, 4, work, 4 - place.core * 4, half),
        ("x", twos, 2, work, fours + 2 - place.x * 2, quarter),
        ("y", one, 1, work, twos + 1 - place.y, eighth),
        ("z", one, 1, None, None, None),
        ("y", one, 1, total_ref, twos + 1 - place.y, None),
        ("x", twos, 2, total_ref, fours + 2 - place.x * 2, None),
        ("core", fours, 4, total_ref, 4 - place.core * 4, None),
    ]

    def push(level, source, target, dim):
        pltpu.make_async_remote_copy(
            src_ref=source,
            dst_ref=target,
            send_sem=sent.at[level],
            recv_sem=got.at[level],
            device_id=place.neighbour(dim, 0),
            device_id_type=MESH,
        ).start()

    def along(other):
        return pltpu.make_async_remote_copy(
            src_ref=line.at[place.z],
            dst_ref=line.at[place.z],
            send_sem=sent.at[7 + other],
            recv_sem=got.at[7 + place.z],
            device_id=(other * 2 + place.core, place.ctx),
            device_id_type=MESH,
        )

    def send(level):
        dim, low, size, buffer, away, room = swaps[level]
        if level == 0:
            work[...] = small_ref[...]
        if dim == "z":
            line[place.z] = work[one]
            for other in range(depth):
                pl.when(place.z != other)(along(other).start)
        elif room is not None:
            push(level, buffer.at[pl.ds(away, size)], room, dim)
        else:
            push(level, buffer.at[pl.ds(low, size)], buffer.at[pl.ds(low, size)], dim)

    def finish(level):
        dim, low, size, buffer, away, room = swaps[level]
        if dim == "z":
            for other in range(depth):
                pl.when(place.z != other)(
                    functools.partial(drain, line.at[other], got.at[7 + other])
                )
            value = line[0]
            for other in range(1, depth):
                value = value + line[other]
            total_ref[one] = value
        elif room is not None:
            drain(room, got.at[level])
            work[pl.ds(low, size)] += room[...]
        else:
            drain(buffer.at[pl.ds(away, size)], got.at[level])
        if level + 1 < len(swaps):
            send(level + 1)

    def close():
        for level, (dim, _, size, _, _, _) in enumerate(swaps):
            if dim == "z":
                for other in range(depth):
                    pl.when(place.z != other)(
                        functools.partial(drain, line.at[other], sent.at[7 + other])
                    )
            else:
                drain(work.at[pl.ds(0, size)], sent.at[level])

    return (send, finish, close)


def scatter_kernel(extents, parts, order, small, border, *refs):
    left_ref, right_ref, refs = (refs[0], refs[1], refs[2:])
    if small:
        small_ref, out_ref, total_ref, refs = (refs[0], refs[1], refs[2], refs[3:])
    else:
        out_ref, refs = (refs[0], refs[1:])
    count = len(parts)
    stages, sides, owns, rooms, accs = [refs[i * count : (i + 1) * count] for i in range(5)]
    side_got, child_got, side_sent, sent = refs[5 * count : 5 * count + 4]
    place = Place(extents)
    chips = extents["z"] * extents["y"] * extents["x"]
    high, columns = (left_ref.shape[1], right_ref.shape[1])
    rank = {}
    for part, (_, _, dims) in enumerate(parts):
        for slot in route_slots(dims, extents):
            rank[part, slot_key(slot)] = len(rank)
    place.greet(whole=small)
    if small:
        send, finish, close = small_steps(place, small_ref, total_ref, *refs[5 * count + 4 :])
        send(0)

    def fill(shard, chip, targets):
        left = left_ref[shard].astype(jnp.float32)
        line = lax.broadcasted_iota(jnp.int32, (high, 1), 0) + shard * high
        early = jnp.where(line < border, 1.0, 0.0)
        wide = jnp.concatenate([left * early, left * (1.0 - early)], axis=1).astype(jnp.bfloat16)

        def one(turn, carry):
            cut = pl.ds(pl.multiple_of(turn * 256, 256), 256)
            value = dot(wide, right_ref[:, cut]).astype(jnp.bfloat16)
            for part, (start, rows, _) in enumerate(parts):
                targets[part].at[chip][:, cut] = value[start : start + rows]
            return carry

        lax.fori_loop(0, columns // 256, one, 0)

    def far_first(z, turn):
        depth = extents["z"]
        return depth - 1 - turn if z < depth // 2 else turn

    def spread(turn, flip_y, flip_x):
        depth = extents["z"]
        z = jnp.where(place.z < depth // 2, depth - 1 - turn, turn)
        y = 1 - place.y if flip_y else place.y
        x = 1 - place.x if flip_x else place.x
        chip = (z * 2 + y) * 2 + x
        fill(((z * 2 + 1 - place.core) * 2 + y) * 2 + x, chip, stages)
        for part in range(count):
            pltpu.make_async_remote_copy(
                src_ref=stages[part].at[chip],
                dst_ref=sides[part].at[chip],
                send_sem=side_sent.at[part],
                recv_sem=side_got.at[part, chip],
                device_id=place.neighbour("core", 0),
                device_id_type=MESH,
            ).start()
        fill(((z * 2 + place.core) * 2 + y) * 2 + x, chip, owns)

    due = {}
    for z in range(extents["z"]):
        for turn in range(extents["z"]):
            ahead = far_first(z, turn) - z
            for i, (_, key) in enumerate(order):
                if key[0] == ahead:
                    name = (turn,) + key[1:]
                    due[name] = min(due.get(name, i), i)
    due = sorted((when, name) for name, when in due.items())

    def room_index(part, slot, dim, side):
        z, y, x = place.source(slot)
        spot = {"z": z, "y": y, "x": x}
        base, names = child_rooms(parts[part][2], extents)[0][dim, side]
        index = 0
        for name in names:
            index = index * extents[name] + spot[name]
        return base + index

    def by_columns(body):
        def one(turn, carry):
            body(pl.ds(pl.multiple_of(turn * 128, 128), 128))
            return carry

        lax.fori_loop(0, columns // 128, one, 0)

    def merge(part, key):
        start, rows, dims = parts[part]
        slot = dict(zip(("z", "y", "x"), key))
        number = rank[part, key]

        def step():
            chip = place.chip_index(slot)
            side, own, acc = (sides[part].at[chip], owns[part].at[chip], accs[part])
            found = [
                (
                    rooms[part].at[room_index(part, slot, dim, sign)],
                    child_got.at[number, CHILD_SEM[dim, sign]],
                    place.has(dim, sign),
                )
                for dim, sign, _ in route_children(slot, dims, extents)
            ]
            sure = [room for room, _, near in found if near is None]
            maybe = [one for one in found if one[2] is not None]
            drain(side, side_got.at[part, chip])
            for room, got, near in found:
                if near is None:
                    drain(room, got)
            last = key == (0, 0, 0)

            def settle(value, cut):
                if maybe:
                    acc[:, cut] = value
                elif last:
                    out_ref[pl.ds(start, rows), cut] = value
                else:
                    side[:, cut] = value.astype(jnp.bfloat16)

            def base(cut):
                value = own[:, cut].astype(jnp.float32) + side[:, cut].astype(jnp.float32)
                for room in sure:
                    value = value + room[:, cut].astype(jnp.float32)
                settle(value, cut)

            by_columns(base)
            for room, got, near in maybe:

                def take(room=room, got=got):
                    drain(room, got)

                    def more(cut):
                        acc[:, cut] += room[:, cut].astype(jnp.float32)

                    by_columns(more)

                pl.when(near)(take)
            if maybe:

                def close_up(cut):
                    if last:
                        out_ref[pl.ds(start, rows), cut] = acc[:, cut]
                    else:
                        side[:, cut] = acc[:, cut].astype(jnp.bfloat16)

                by_columns(close_up)
            if last:
                return
            dim, sign, seen, parent = route_parent(slot)(dims)
            pltpu.make_async_remote_copy(
                src_ref=side,
                dst_ref=rooms[part].at[room_index(part, slot, dim, seen)],
                send_sem=sent.at[part],
                recv_sem=child_got.at[rank[part, slot_key(parent)], CHILD_SEM[dim, seen]],
                device_id=place.neighbour(dim, sign),
                device_id_type=MESH,
            ).start()

        guarded(place.valid(slot), step)

    finishes = [2, 8, 14, 22, 34, 46, 60]
    for i, one in enumerate(order):
        while due and due[0][0] <= i + 6:
            spread(*due.pop(0)[1])
        merge(*one)
        if small and i * 84 // len(order) in finishes:
            finish(finishes.index(i * 84 // len(order)))
    if small:
        close()
    for part in range(count):
        drain(stages[part], side_sent.at[part])
        drain(sides[part].at[pl.ds(0, chips - 1)], sent.at[part])


def scattered(left, right, border, small, extents, number):
    total, rows, depth = left.shape
    columns = right.shape[1]
    chips = total // 2
    parts = row_parts(rows)
    order = list(reversed(route_order(parts, extents)))
    slots = len(order)
    vmem = pl.BlockSpec(memory_space=pltpu.VMEM)
    args = (left, right)
    outs = [jax.ShapeDtypeStruct((rows, columns), jnp.float32)]
    scratch = (
        [pltpu.VMEM((chips, size, columns), jnp.bfloat16) for _, size, _ in parts] * 3
        + [
            pltpu.VMEM((child_rooms(dims, extents)[1], size, columns), jnp.bfloat16)
            for _, size, dims in parts
        ]
        + [pltpu.VMEM((size, columns), jnp.float32) for _, size, _ in parts]
        + [
            pltpu.SemaphoreType.DMA((len(parts), chips)),
            pltpu.SemaphoreType.DMA((slots, 4)),
            pltpu.SemaphoreType.DMA((len(parts),)),
            pltpu.SemaphoreType.DMA((len(parts),)),
        ]
    )
    if small is not None:
        args = args + (small,)
        outs.append(jax.ShapeDtypeStruct(small.shape, jnp.float32))
        depth = extents["z"]
        sizes = [8, 4, 2, 1, depth]
        scratch = scratch + [
            pltpu.VMEM((size,) + small.shape[1:], jnp.float32) for size in sizes
        ]
        scratch = scratch + [pltpu.SemaphoreType.DMA((7 + depth,))] * 2
    return pl.pallas_call(
        functools.partial(scatter_kernel, extents, parts, order, small is not None, border),
        out_shape=outs,
        in_specs=[vmem] * len(args),
        out_specs=[vmem] * len(outs),
        scratch_shapes=scratch,
        compiler_params=pltpu.CompilerParams(
            collective_id=number, has_side_effects=True, vmem_limit_bytes=56 * 1024 * 1024
        ),
    )(*args)


def routed():
    return lax.axis_size("ctx") == 4 and lax.axis_size("dp") % 2 == 0


def route_extents():
    return {"z": lax.axis_size("dp") // 2, "y": 2, "x": 2}


def all_rows(shard, number):
    if routed():
        return gathered(shard, route_extents(), number)
    return lax.all_gather(shard, ("dp", "ctx"), axis=0, tiled=True)


def owner_sums(first_left, first_right, second_left, second_right, small, number):
    if not routed():
        grad = to_owners(owner_rows(first_left, first_right, second_left, second_right))
        return (grad, None if small is None else lax.psum(small, ("dp", "ctx")))
    left = jnp.concatenate([first_left.T, second_left.T])
    border = first_left.shape[1]
    devices = lax.axis_size("dp") * lax.axis_size("ctx")
    left = left.reshape(devices, left.shape[0] // devices, left.shape[1])
    right = jnp.concatenate([first_right, second_right])
    if small is None:
        return (scattered(left, right, border, None, route_extents(), number)[0], None)
    extent = small.shape[0]
    rows = -(-extent // 8192) * 8
    packed = jnp.pad(small, (0, rows * 1024 - extent)).reshape(8, rows, 128)
    grad, totals = scattered(left, right, border, packed, route_extents(), number)
    return (grad, totals.reshape(-1)[:extent])


def shifted(shard, by):
    return passed_along(shard, "ctx", by)


def per_device(
    inputs,
    segments,
    cotangent,
    mixer_params,
    mixer_first,
    mixer_second,
    feed_params,
    feed_first,
    feed_second,
    small_params,
    small_first,
    small_second,
):
    mixer_weights = all_rows(mixer_params.astype(jnp.bfloat16), 0)
    feed_half, mixer_weights = lax.optimization_barrier(
        (feed_params.astype(jnp.bfloat16), mixer_weights)
    )
    feed_weights = all_rows(feed_half, 1)
    conv_weight, gain_first, gain_second, out_gain, gate_rows, decay_log, decay_bias = unpack_small(
        small_params
    )
    channels = 2 * H * DK + H * DV
    input_rows = channels + H * DV
    margin = CONV - 1
    in_weight = mixer_weights[:input_rows]
    out_weight = mixer_weights[input_rows:]
    up_weight = feed_weights[: 2 * FF]
    down_weight = feed_weights[2 * FF :]
    tokens_here = inputs[0]
    cotangent_here = cotangent[0]
    token_count = tokens_here.shape[0]
    position = lax.axis_index("ctx") * token_count
    segment_padded = jnp.concatenate([jnp.full((margin,), -1, jnp.int32), segments[0]])
    segment_wide = lax.dynamic_slice_in_dim(segment_padded, position, token_count + margin)
    segment_ids = segment_wide[margin:]
    segment_before = segment_wide[margin - 1]
    inverse_first = lax.rsqrt(
        jnp.mean(tokens_here * tokens_here, axis=-1, keepdims=True) + EPS_NORM
    )
    normed = (tokens_here * inverse_first * gain_first).astype(jnp.bfloat16)
    gate_half = gate_rows.astype(jnp.bfloat16)
    logits = jnp.einsum("td,rd->tr", normed, gate_half, preferred_element_type=jnp.float32)
    rim_normed = shifted(normed[token_count - margin :], 1)
    projected = jnp.einsum(
        "td,rd->tr",
        jnp.concatenate([normed, rim_normed]),
        in_weight,
        preferred_element_type=jnp.float32,
    )
    rim_rows = projected[token_count:, :channels].astype(jnp.bfloat16)
    projected = projected[:token_count]
    conv_input = projected[:, :channels].astype(jnp.bfloat16)
    gate_pre = projected[:, channels:]
    extended = jnp.concatenate([rim_rows, conv_input]).astype(jnp.float32)

    active, active_back = jax.vjp(
        lambda wide, taps: active_rows(wide, taps, segment_wide), extended, conv_weight
    )
    span = min(SPAN, token_count)
    count = token_count // span
    scalars, scalars_back = jax.vjp(
        lambda *args: block_scalars(*args, segment_ids, segment_before, span),
        logits[:, :H],
        logits[:, H:],
        decay_log,
        decay_bias,
    )
    beta, running, carried, last = scalars
    segment_rows = jnp.broadcast_to(
        segment_ids.astype(jnp.float32).reshape(1, count, span), beta.shape
    )
    blank = jnp.zeros_like(beta)
    row_pack = jnp.stack(
        [beta, running, segment_rows, carried, last, blank, blank, blank], axis=2
    )
    column_pack = jnp.swapaxes(row_pack, 2, 3)
    groups = H // GROUP
    key_blocks = H * DK // (GROUP * DK)
    value_start = 2 * H * DK // (GROUP * DV)
    query_spec = pl.BlockSpec((span, GROUP * DK), lambda c, g: (c, g))
    key_spec = pl.BlockSpec((span, GROUP * DK), lambda c, g: (c, g + key_blocks))
    value_spec = pl.BlockSpec((span, GROUP * DV), lambda c, g: (c, g + value_start))
    wide_spec = pl.BlockSpec((span, GROUP * DV), lambda c, g: (c, g))
    row_spec = pl.BlockSpec((GROUP, 1, 8, span), lambda c, g: (g, c, 0, 0))
    column_spec = pl.BlockSpec((GROUP, 1, span, 8), lambda c, g: (g, c, 0, 0))
    inverse_spec = pl.BlockSpec((1, GROUP, span, span), lambda c, g: (c, g, 0, 0))
    square_spec = pl.BlockSpec((1, GROUP, DK, DK), lambda c, g: (c, g, 0, 0))
    state_spec = pl.BlockSpec((1, GROUP, DK, DV), lambda c, g: (c, g, 0, 0))
    gain_spec = pl.BlockSpec((1, DV), lambda c, g: (0, 0))
    key_out = ((token_count, H * DK), jnp.float32)
    value_out = ((token_count, H * DV), jnp.float32)
    state_out = ((count, H, DK, DV), jnp.float32)
    grid = (count, groups)
    inverse, w_part, u_part, r_part, o_part, transfers, offsets = kernel_call(
        block_kernel,
        grid,
        (active, active, active, row_pack, column_pack),
        [query_spec, key_spec, value_spec, row_spec, column_spec],
        [
            ((count, H, span, span), jnp.float32),
            key_out,
            value_out,
            key_out,
            value_out,
            ((count, H, DK, DK), jnp.float32),
            state_out,
        ],
        [inverse_spec, query_spec, wide_spec, query_spec, wide_spec, square_spec, state_spec],
    )

    def advance(left, right):
        return jnp.einsum(
            "hij,hjw->hiw", left, right, precision=CORE, preferred_element_type=jnp.float32
        )

    def advance_back(left, right):
        return jnp.einsum(
            "hji,hjw->hiw", left, right, precision=CORE, preferred_element_type=jnp.float32
        )

    transfer, offset_state = (transfers[0], offsets[0])
    for block in range(1, count):
        transfer = advance(transfers[block], transfer)
        offset_state = advance(transfers[block], offset_state) + offsets[block]
    ring = lax.axis_size("ctx")
    transfer_half = transfer.astype(jnp.bfloat16)
    offset_half = offset_state.astype(jnp.bfloat16)
    befores = [
        (shifted(transfer_half, by), shifted(offset_half, by)) for by in range(1, ring)
    ]
    state_in = jnp.zeros((H, DK, DV), jnp.float32)
    for transfer_there, offset_there in reversed(befores):
        state_in = advance(transfer_there.astype(jnp.float32), state_in) + offset_there
    states = [state_in]
    for block in range(count - 1):
        states.append(advance(transfers[block], states[-1]) + offsets[block])
    states = jnp.stack(states)
    gain_row = out_gain.reshape(1, DV)
    recurrent_out, mix_half = kernel_call(
        output_kernel,
        grid,
        (r_part, o_part, states, gate_pre, gain_row),
        [query_spec, wide_spec, state_spec, wide_spec, gain_spec],
        [value_out, ((token_count, H * DV), jnp.bfloat16)],
        [wide_spec, wide_spec],
    )
    afters = [shifted(transfer_half, -by) for by in range(1, ring)]
    hidden = tokens_here + jnp.dot(mix_half, out_weight, preferred_element_type=jnp.float32)
    inverse_second = lax.rsqrt(jnp.mean(hidden * hidden, axis=-1, keepdims=True) + EPS_NORM)
    hidden_normed = (hidden * inverse_second * gain_second).astype(jnp.bfloat16)
    gate_up = jnp.einsum("td,rd->tr", hidden_normed, up_weight, preferred_element_type=jnp.float32)
    gate_part = gate_up[:, :FF]
    up_part = gate_up[:, FF:]
    middle = (jax.nn.silu(gate_part) * up_part).astype(jnp.bfloat16)
    result = hidden + jnp.dot(middle, down_weight, preferred_element_type=jnp.float32)
    cotangent_half = cotangent_here.astype(jnp.bfloat16)
    grad_middle = jnp.einsum(
        "td,fd->tf", cotangent_half, down_weight, preferred_element_type=jnp.float32
    )
    sigmoid_gate = jax.nn.sigmoid(gate_part)
    grad_gate = (
        grad_middle * up_part * (sigmoid_gate + gate_part * sigmoid_gate * (1.0 - sigmoid_gate))
    )
    grad_up = grad_middle * gate_part * sigmoid_gate
    grad_gate_up = jnp.concatenate([grad_gate, grad_up], axis=1).astype(jnp.bfloat16)
    grad_hidden_normed = jnp.dot(grad_gate_up, up_weight, preferred_element_type=jnp.float32)
    grad_hidden = cotangent_here + norm_back(
        hidden, inverse_second, gain_second, grad_hidden_normed
    )
    grad_gain_second = jnp.sum(grad_hidden_normed * hidden * inverse_second, axis=0)
    grad_hidden_half = grad_hidden.astype(jnp.bfloat16)
    feed_grad, _ = owner_sums(grad_gate_up, hidden_normed, middle, cotangent_half, None, 2)
    grad_mix = jnp.einsum(
        "td,rd->tr", grad_hidden_half, out_weight, preferred_element_type=jnp.float32
    )
    partial_spec = pl.BlockSpec((1, 1, DV), lambda c, g: (c * groups + g, 0, 0))
    grad_recurrent, grad_gate_pre, gain_parts, locals_back = kernel_call(
        gate_back_kernel,
        grid,
        (grad_mix, recurrent_out, gate_pre, gain_row, r_part),
        [wide_spec, wide_spec, wide_spec, gain_spec, query_spec],
        [value_out, value_out, ((count * groups, 1, DV), jnp.float32), state_out],
        [wide_spec, wide_spec, partial_spec, state_spec],
    )
    grad_out_gain = jnp.sum(gain_parts, axis=(0, 1))
    local_part = locals_back[count - 1]
    for block in range(count - 2, -1, -1):
        local_part = advance_back(transfers[block], local_part) + locals_back[block]
    local_half = local_part.astype(jnp.bfloat16)
    local_afters = [shifted(local_half, -by) for by in range(1, ring)]
    state_grad = jnp.zeros((H, DK, DV), jnp.float32)
    for transfer_there, local_there in reversed(list(zip(afters, local_afters))):
        state_grad = advance_back(transfer_there.astype(jnp.float32), state_grad) + local_there
    nexts = [state_grad]
    for block in range(count - 1, 0, -1):
        nexts.append(advance_back(transfers[block], nexts[-1]) + locals_back[block])
    nexts = jnp.stack(nexts[::-1])
    grad_q, grad_k, grad_v, grad_row_pack, grad_column_pack = kernel_call(
        block_back_kernel,
        grid,
        (
            active,
            active,
            active,
            row_pack,
            column_pack,
            inverse,
            w_part,
            u_part,
            states,
            grad_recurrent,
            nexts,
        ),
        [
            query_spec,
            key_spec,
            value_spec,
            row_spec,
            column_spec,
            inverse_spec,
            query_spec,
            wide_spec,
            state_spec,
            wide_spec,
            state_spec,
        ],
        [key_out, key_out, value_out, (row_pack.shape, jnp.float32), (column_pack.shape, jnp.float32)],
        [query_spec, query_spec, wide_spec, row_spec, column_spec],
    )
    grad_pack = grad_row_pack + jnp.swapaxes(grad_column_pack, 2, 3)
    grad_beta_logit, grad_alpha_logit, grad_decay_log, grad_decay_bias = scalars_back(
        (grad_pack[:, :, 0], grad_pack[:, :, 1], grad_pack[:, :, 3], grad_pack[:, :, 4])
    )
    grad_wide, grad_conv = active_back(jnp.concatenate([grad_q, grad_k, grad_v], axis=1))
    back_rim = passed_along(grad_wide[:margin].astype(jnp.bfloat16), "ctx", -1).astype(jnp.float32)
    grad_conv_input = grad_wide[margin:]
    grad_conv_input = jnp.concatenate(
        [
            grad_conv_input[: token_count - margin],
            grad_conv_input[token_count - margin :] + back_rim,
        ]
    )
    grad_projected = jnp.concatenate([grad_conv_input, grad_gate_pre], axis=1).astype(jnp.bfloat16)
    grad_logits = jnp.concatenate([grad_beta_logit, grad_alpha_logit], axis=1).astype(jnp.bfloat16)
    grad_normed = jnp.dot(grad_projected, in_weight, preferred_element_type=jnp.float32)
    grad_normed = grad_normed + jnp.dot(grad_logits, gate_half, preferred_element_type=jnp.float32)
    grad_inputs = grad_hidden + norm_back(tokens_here, inverse_first, gain_first, grad_normed)
    grad_gain_first = jnp.sum(grad_normed * tokens_here * inverse_first, axis=0)
    gate_grad = jnp.einsum("tr,td->rd", grad_logits, normed, preferred_element_type=jnp.float32)
    small_local = jnp.concatenate(
        [
            grad_conv.reshape(-1),
            grad_gain_first,
            grad_gain_second,
            grad_out_gain,
            gate_grad.reshape(-1),
            grad_decay_log,
            grad_decay_bias,
        ]
    )
    mixer_grad, small_grad = owner_sums(
        grad_projected, normed, mix_half, grad_hidden_half, small_local, 3
    )
    mixer_new, mixer_moment, mixer_square = adamw(
        mixer_params, mixer_grad, mixer_first, mixer_second
    )
    feed_new, feed_moment, feed_square = adamw(feed_params, feed_grad, feed_first, feed_second)
    small_new, small_moment, small_square = adamw(
        small_params, small_grad, small_first, small_second
    )
    return (
        result[None],
        grad_inputs[None],
        mixer_grad,
        feed_grad,
        small_grad,
        mixer_new,
        mixer_moment,
        mixer_square,
        feed_new,
        feed_moment,
        feed_square,
        small_new,
        small_moment,
        small_square,
    )


def solution(mesh):
    in_specs = (
        P("dp", "ctx", None),
        P("dp", None),
        P("dp", "ctx", None),
        P(("dp", "ctx"), None),
        P(("dp", "ctx"), None),
        P(("dp", "ctx"), None),
        P(("dp", "ctx"), None),
        P(("dp", "ctx"), None),
        P(("dp", "ctx"), None),
        P(),
        P(),
        P(),
    )
    out_specs = (
        P("dp", "ctx", None),
        P("dp", "ctx", None),
        P(("dp", "ctx"), None),
        P(("dp", "ctx"), None),
        P(),
        P(("dp", "ctx"), None),
        P(("dp", "ctx"), None),
        P(("dp", "ctx"), None),
        P(("dp", "ctx"), None),
        P(("dp", "ctx"), None),
        P(("dp", "ctx"), None),
        P(),
        P(),
        P(),
    )
    return jax.shard_map(
        per_device, mesh=mesh, in_specs=in_specs, out_specs=out_specs, check_vma=False
    )
```
